128 devices in a mesh: ctx: 32 (over y, x_lo, z), tp: 4 (over x_hi, core).
Axes of the slice: x: 4 (x_hi: 2, x_lo: 2; x = x_hi * 2 + x_lo), y: 4, z: 4, core: 2. Of those that a mesh axis runs over, the one named last changes fastest.
Arguments:
- query_one: bfloat16 [8192, 8192], P('ctx', 'tp'), may hold values from -6 to 6
- key_one: bfloat16 [8192, 8192], P('ctx', 'tp'), may hold values from -6 to 6
- value_one: bfloat16 [8192, 8192], P('ctx', 'tp'), may hold values from -6 to 6
- residual_in: bfloat16 [8192, 8192], P('ctx', 'tp'), may hold values from -50 to 50
- medium_taps: bfloat16 [128, 8192], P(None, 'tp'), may hold values from -0.5 to 0.5
- skip_one: float32 [8192], P('tp'), may hold values from -4 to 4
- norm_gain: float32 [8192], P('tp'), may hold values from 0.5 to 1.5
- query_two: bfloat16 [8192, 8192], P('ctx', 'tp'), may hold values from -6 to 6
- key_two: bfloat16 [8192, 8192], P('ctx', 'tp'), may hold values from -6 to 6
- residues: float32 [16, 8192], P(None, 'tp'), may hold values from -2 to 2
- decay_rates: float32 [16, 8192], P(None, 'tp'), may hold values from 0.00012207031 to 0.03
- skip_two: float32 [8192], P('tp'), may hold values from -4 to 4
Outputs:
- residual_out: bfloat16 [8192, 8192], P('ctx', 'tp')
- long_output: bfloat16 [8192, 8192], P('ctx', 'tp')
The draws below stay inside these ranges and needn't reach their ends.
All inputs are finite; a program needn't handle non-finite values.
Results may differ from the reference program's by a relative error of at most 0.013.
Values may be sent and summed in bfloat16 or wider, within the bound.
No kernel may reach another device: no remote copies, remote signals or barrier semaphores. Data moves between devices by JAX's collectives and lax.ppermute only.
A program may use at most 128 MiB of HBM per device.

```python
import math
import jax
import jax.numpy as jnp
from jax import lax

D = 8192
TAPS = 128
MODES = 16
TOKENS = 8192


def draw_residual_in(key, part):
    key_rows, key_cols, key_base = jax.random.split(key, 3)
    row_scale = jnp.exp(jax.random.uniform(key_rows, (TOKENS, 1), jnp.float32, math.log(0.3), math.log(3.0)))
    column_ramp = 0.5 * jnp.exp(math.log(3.0) * jnp.arange(D).astype(jnp.float32) / (D - 1))
    column_rough = jnp.exp(jax.random.uniform(key_cols, (D,), jnp.float32, -0.6, 0.6))
    base_values = jax.random.normal(key_base, (TOKENS, D), jnp.float32)
    base_values = jnp.clip(base_values, -6.0, 6.0)
    return jnp.clip(base_values * row_scale * column_ramp * column_rough, -50.0, 50.0).astype(jnp.bfloat16)


def steps_of(own_key, extent, pieces, smallest, largest):
    level = 1.0
    for position, parts in pieces:
        heights = jax.random.uniform(jax.random.fold_in(jax.random.fold_in(own_key, 6), position), (parts,), jnp.float32, smallest / len(pieces), largest / len(pieces))
        level = level * jnp.repeat(jnp.exp(heights), extent[position] // parts).reshape((-1,) + (1,) * (len(extent) - 1 - position))
    return level


def noise(stream_key, extent, spread, limit, cuts=(), held_as=jnp.bfloat16):
    values = jax.random.normal(stream_key, extent, jnp.float32) * spread
    if len(cuts) > 0:
        values = steps_of(stream_key, extent, cuts, -0.22, 0.18) * values
    return jnp.clip(values, min=-limit, max=limit).astype(held_as)


def setup_inputs(seed: int = 0) -> dict:
    seeds = jax.random.split(jax.random.key(seed), 13)
    query_one = noise(seeds[0], (TOKENS, D), 1.0, 6.0, ((0, 32), (1, 4)))
    key_one = noise(seeds[1], (TOKENS, D), 1.0, 6.0, ((0, 32), (1, 4)))
    value_one = noise(seeds[2], (TOKENS, D), 1.0, 6.0, ((0, 32), (1, 4)))
    residual_in = draw_residual_in(jax.random.fold_in(seeds[12], 71), 0)
    medium_taps = noise(seeds[4], (TAPS, D), TAPS ** -0.5, 0.5, ((1, 4),))
    skip_one = noise(seeds[5], (D,), 1.0, 4.0, ((0, 4),), jnp.float32)
    norm_gain = jnp.clip(1.0 + 0.1 * jax.random.normal(seeds[6], (D,), jnp.float32), 0.5, 1.5)
    query_two = noise(seeds[7], (TOKENS, D), 1.0, 6.0, ((0, 32), (1, 4)))
    key_two = noise(seeds[8], (TOKENS, D), 1.0, 6.0, ((0, 32), (1, 4)))
    residues = noise(seeds[9], (MODES, D), 0.35, 2.0, ((1, 4),), jnp.float32)
    decay_rates = jnp.clip(jnp.exp(math.log(0.03) - 5.5043554 * jax.random.uniform(seeds[10], (MODES, D), jnp.float32) ** steps_of(seeds[10], (MODES, D), ((1, 4),), -0.2, 0.2)), 0.00012207031, 0.03)
    skip_two = noise(seeds[11], (D,), 1.0, 4.0, ((0, 4),), jnp.float32)
    return dict(query_one=query_one, key_one=key_one, value_one=value_one, residual_in=residual_in, medium_taps=medium_taps, skip_one=skip_one, norm_gain=norm_gain, query_two=query_two, key_two=key_two, residues=residues, decay_rates=decay_rates, skip_two=skip_two)


def modal_taps(local_residues, local_rates, offsets):
    running = jnp.zeros((offsets.shape[0], local_residues.shape[1]), jnp.float32)
    for mode_index in range(local_residues.shape[0]):
        running = running + local_residues[mode_index] * jnp.sqrt(local_rates[mode_index]) * jnp.exp(-local_rates[mode_index] * offsets[:, None])
    return running

def reference(query_one, key_one, value_one, residual_in, medium_taps, skip_one, norm_gain, query_two, key_two, residues, decay_rates, skip_two):
    product_one = (key_one.astype(jnp.float32) * value_one.astype(jnp.float32)).astype(jnp.bfloat16)
    padded = jnp.concatenate([jnp.zeros((TAPS - 1, D), jnp.bfloat16), product_one], axis=0)

    def add_tap(tap_index, running):
        shifted = lax.dynamic_slice_in_dim(padded, (TAPS - 1 - tap_index).astype(jnp.int32), TOKENS, 0)
        return running + medium_taps[tap_index].astype(jnp.float32) * shifted.astype(jnp.float32)
    filtered = lax.fori_loop(0, TAPS, add_tap, jnp.zeros((TOKENS, D), jnp.float32))
    residual_out = (residual_in.astype(jnp.float32) + query_one.astype(jnp.float32) * (filtered + skip_one * product_one.astype(jnp.float32))).astype(jnp.bfloat16)
    widened = residual_out.astype(jnp.float32)
    mean_sq = lax.optimization_barrier(jnp.mean(widened * widened, axis=1, keepdims=True))
    value_two = (key_two.astype(jnp.float32) * widened * lax.rsqrt(mean_sq + 1e-05) * norm_gain).astype(jnp.bfloat16).astype(jnp.float32)

    def convolve_block(block_index):
        start_col = (block_index * 256).astype(jnp.int32)
        signal = lax.dynamic_slice_in_dim(value_two, start_col, 256, 1)
        local_residues = lax.dynamic_slice_in_dim(residues, start_col, 256, 1)
        local_rates = lax.dynamic_slice_in_dim(decay_rates, start_col, 256, 1)
        offsets = jnp.arange(TOKENS).astype(jnp.float32)
        taps_long = modal_taps(local_residues, local_rates, offsets)
        product_spectrum = jnp.fft.rfft(signal, n=2 * TOKENS, axis=0) * jnp.fft.rfft(taps_long, n=2 * TOKENS, axis=0)
        return jnp.fft.irfft(product_spectrum, n=2 * TOKENS, axis=0)[:TOKENS]
    blocks = lax.map(convolve_block, jnp.arange(D // 256, dtype=jnp.int32))
    mixed_two = jnp.transpose(blocks, (1, 0, 2)).reshape(TOKENS, D)
    long_output = (query_two.astype(jnp.float32) * (mixed_two + skip_two * value_two)).astype(jnp.bfloat16)
    return (residual_out, long_output)
```

```python
import functools
import math

import jax
import jax.numpy as jnp
import numpy as np
from jax import lax
from jax.experimental import pallas as pl
from jax.experimental.pallas import tpu as pltpu
from jax.sharding import PartitionSpec as P

HALF = 128
LANES = 128
SUB = 8


def split_table(table):
    upper = table.astype(jnp.bfloat16)
    lower = (table - upper.astype(np.float64)).astype(jnp.bfloat16)
    return upper, lower


def transform_tables(count):
    half = count // 2
    freq = np.arange(half)[:, None]
    time = np.arange(count)[None, :]
    angle = 2.0 * math.pi * ((freq * time) % count) / count
    even = np.cos(angle)
    odd = -np.sin(angle)
    odd[0] = np.where(np.arange(count) % 2 == 0, 1.0, -1.0)
    forward = np.concatenate([even, odd], axis=0)
    weight = np.full((half, 1), 2.0 / count)
    weight[0] = 1.0 / count
    backward = np.concatenate([even * weight, odd * weight], axis=0).T[half:]
    return forward, backward


def dot32(left, right):
    return jnp.dot(left, right, preferred_element_type=jnp.float32)


def filter_kernel(
    before_ref,
    here_ref,
    taps_ref,
    query_ref,
    resid_ref,
    skip_ref,
    fwd_ref,
    bwd_ref,
    out_ref,
    square_ref,
    total_ref,
):
    step = pl.program_id(0)
    count = 2 * HALF
    here = here_ref[...]
    signal = jnp.concatenate([before_ref[...], here], axis=0)
    both = dot32(fwd_ref[...], signal)
    spec = both[:count] + both[count:]
    both_taps = dot32(fwd_ref[:, :HALF], taps_ref[...])
    spec_taps = both_taps[:count] + both_taps[count:]
    sig_even, sig_odd = spec[:HALF], spec[HALF:]
    tap_even, tap_odd = spec_taps[:HALF], spec_taps[HALF:]
    first = lax.broadcasted_iota(jnp.int32, tap_even.shape, 0) == 0
    tap_cross = jnp.where(first, 0.0, tap_odd)
    tap_last = jnp.where(first, tap_odd, tap_even)
    joint = jnp.concatenate(
        [
            sig_even * tap_even - sig_odd * tap_cross,
            sig_even * tap_cross + sig_odd * tap_last,
        ],
        axis=0,
    )
    joint_hi = joint.astype(jnp.bfloat16)
    joint_lo = (joint - joint_hi.astype(jnp.float32)).astype(jnp.bfloat16)
    back = dot32(bwd_ref[...], joint_hi)
    filtered = back[:HALF] + back[HALF:] + dot32(bwd_ref[:HALF], joint_lo)
    mixed = filtered + skip_ref[...] * here.astype(jnp.float32)
    result = (
        resid_ref[...].astype(jnp.float32) + query_ref[...].astype(jnp.float32) * mixed
    ).astype(jnp.bfloat16)
    out_ref[...] = result
    wide = result.astype(jnp.float32)
    squares = wide * wide
    part = squares[:, :LANES]
    for lane_block in range(1, squares.shape[1] // LANES):
        part = part + squares[:, lane_block * LANES : (lane_block + 1) * LANES]

    @pl.when(step == 0)
    def _():
        total_ref[...] = part

    @pl.when(step > 0)
    def _():
        total_ref[...] = total_ref[...] + part

    @pl.when(step == pl.num_programs(0) - 1)
    def _():
        summed = jnp.sum(total_ref[...].T, axis=0, keepdims=True)
        square_ref[...] = jnp.broadcast_to(summed, square_ref.shape)


def medium_block(before, here, taps, query, resid, skip, tables, row_block, width=512):
    channels = here.shape[1]
    forward, backward = tables
    rows = pl.BlockSpec((HALF, width), lambda c: (0, c))
    own = pl.BlockSpec((HALF, width), lambda c: (row_block, c))
    return pl.pallas_call(
        filter_kernel,
        grid=(channels // width,),
        in_specs=[
            rows,
            rows,
            rows,
            own,
            own,
            pl.BlockSpec((1, width), lambda c: (0, c)),
            pl.BlockSpec(forward.shape, lambda c: (0, 0)),
            pl.BlockSpec(backward.shape, lambda c: (0, 0)),
        ],
        out_specs=[rows, pl.BlockSpec((SUB, HALF), lambda c: (0, 0))],
        out_shape=[
            jax.ShapeDtypeStruct((HALF, channels), jnp.bfloat16),
            jax.ShapeDtypeStruct((SUB, HALF), jnp.float32),
        ],
        scratch_shapes=[pltpu.VMEM((HALF, LANES), jnp.float32)],
        name="medium",
    )(before, here, taps, query, resid, skip, forward, backward)


def sublane_iota():
    return lax.broadcasted_iota(jnp.int32, (SUB, LANES), 0)


def shifted_down(value, count):
    return jnp.where(sublane_iota() >= count, pltpu.roll(value, count, axis=0), 0.0)


def state_kernel(
    total_channels,
    low_ref,
    high_ref,
    key_ref,
    square_low_ref,
    square_high_ref,
    gain_ref,
    rate_ref,
    value_ref,
    state_ref,
    prefix_ref,
    wide_ref,
):
    rows = key_ref.shape[0]
    steps = rows // SUB
    modes = rate_ref.shape[0]
    gain = gain_ref[...]
    for part, (out_part, square) in enumerate(
        ((low_ref, square_low_ref), (high_ref, square_high_ref))
    ):
        mean = (square[0] + square[1]) / total_channels
        scale = lax.rsqrt(mean + 1e-05)
        scale = jnp.broadcast_to(scale[:1], (HALF, HALF)).T
        window = pl.ds(part * HALF, HALF)
        value = (
            key_ref[window, :].astype(jnp.float32)
            * out_part[...].astype(jnp.float32)
            * scale
            * gain
        ).astype(jnp.bfloat16)
        value_ref[window, :] = value
        wide_ref[window, :] = value.astype(jnp.float32)
    decay = [
        jnp.exp(-jnp.broadcast_to(rate_ref[m : m + 1, :], (SUB, LANES))) for m in range(modes)
    ]
    held = [None] * modes
    for i in range(steps):
        value = wide_ref[pl.ds(i, SUB, stride=steps), :]
        for m in range(modes):
            held[m] = value if i == 0 else held[m] * decay[m] + value
    for m in range(modes):
        rate = jnp.broadcast_to(rate_ref[m : m + 1, :], (SUB, LANES))
        run = held[m]
        for span in (1, 2, 4):
            run = run + jnp.exp(-rate * float(steps * span)) * shifted_down(run, span)
        prefix_ref[0, m] = shifted_down(run, 1)
        state_ref[m // SUB, 0, m % SUB : m % SUB + 1, :] = run[SUB - 1 : SUB]


def local_states(low, high, key, square_low, square_high, gain, rates, total_channels):
    rows, channels = key.shape
    modes = rates.shape[0]
    blocks = channels // LANES
    half = pl.BlockSpec((HALF, LANES), lambda c: (0, c))
    square = pl.BlockSpec((2, SUB, HALF), lambda c: (0, 0, 0))
    full = pl.BlockSpec((rows, LANES), lambda c: (0, c))
    return pl.pallas_call(
        functools.partial(state_kernel, total_channels),
        grid=(blocks,),
        in_specs=[
            half,
            half,
            full,
            square,
            square,
            pl.BlockSpec((1, LANES), lambda c: (0, c)),
            pl.BlockSpec((modes, LANES), lambda c: (0, c)),
        ],
        out_specs=[
            full,
            pl.BlockSpec((modes // SUB, 1, SUB, LANES), lambda c: (0, c, 0, 0)),
            pl.BlockSpec((1, modes, SUB, LANES), lambda c: (c, 0, 0, 0)),
        ],
        out_shape=[
            jax.ShapeDtypeStruct((rows, channels), jnp.bfloat16),
            jax.ShapeDtypeStruct((modes // SUB, blocks, SUB, LANES), jnp.float32),
            jax.ShapeDtypeStruct((blocks, modes, SUB, LANES), jnp.float32),
        ],
        scratch_shapes=[pltpu.VMEM((rows, LANES), jnp.float32)],
        name="states",
    )(low, high, key, square_low, square_high, gain, rates)


def scan_kernel(span, rate_ref, end_ref, start_ref):
    decay = jnp.exp(-rate_ref[...] * span)
    held = jnp.zeros_like(decay)
    for source in range(end_ref.shape[0]):
        start_ref[source] = held
        held = held * decay + end_ref[source]


def scanned(rate_tile, ends, span):
    return pl.pallas_call(
        functools.partial(scan_kernel, float(span)),
        out_shape=jax.ShapeDtypeStruct(ends.shape, ends.dtype),
        name="scan",
    )(rate_tile, ends)


def output_kernel(
    value_ref,
    start_ref,
    prefix_ref,
    rate_ref,
    residue_ref,
    query_ref,
    skip_ref,
    out_ref,
    wide_ref,
    mixed_ref,
):
    rows = value_ref.shape[0]
    steps = rows // SUB
    modes = rate_ref.shape[0]
    wide_ref[...] = value_ref[...].astype(jnp.float32)
    position = sublane_iota().astype(jnp.float32) * float(steps)
    decay, weight, held = [], [], []
    for m in range(modes):
        rate = jnp.broadcast_to(rate_ref[m : m + 1, :], (SUB, LANES))
        factor = jnp.broadcast_to(residue_ref[m : m + 1, :], (SUB, LANES)) * jnp.sqrt(rate)
        start = jnp.broadcast_to(
            start_ref[m // SUB, 0, m % SUB : m % SUB + 1, :], (SUB, LANES)
        )
        decay.append(jnp.exp(-rate))
        weight.append(factor)
        held.append(factor * (prefix_ref[0, m] + jnp.exp(-rate * position) * start))
    for i in range(steps):
        value = wide_ref[pl.ds(i, SUB, stride=steps), :]
        for m in range(modes):
            held[m] = held[m] * decay[m] + weight[m] * value
        terms = list(held)
        while len(terms) > 1:
            terms = [terms[k] + terms[k + 1] for k in range(0, len(terms), 2)]
        mixed_ref[pl.ds(i, SUB, stride=steps), :] = terms[0]
    out_ref[...] = (
        query_ref[...].astype(jnp.float32) * (mixed_ref[...] + skip_ref[...] * wide_ref[...])
    ).astype(jnp.bfloat16)


def long_output(value, starts, prefix, rates, residues, query, skip):
    rows, channels = value.shape
    modes = rates.shape[0]
    blocks = channels // LANES
    full = pl.BlockSpec((rows, LANES), lambda c: (0, c))
    per_mode = pl.BlockSpec((modes, LANES), lambda c: (0, c))
    return pl.pallas_call(
        output_kernel,
        grid=(blocks,),
        in_specs=[
            full,
            pl.BlockSpec((modes // SUB, 1, SUB, LANES), lambda c: (0, c, 0, 0)),
            pl.BlockSpec((1, modes, SUB, LANES), lambda c: (c, 0, 0, 0)),
            per_mode,
            per_mode,
            full,
            pl.BlockSpec((1, LANES), lambda c: (0, c)),
        ],
        out_specs=full,
        out_shape=jax.ShapeDtypeStruct((rows, channels), jnp.bfloat16),
        scratch_shapes=[
            pltpu.VMEM((rows, LANES), jnp.float32),
            pltpu.VMEM((rows, LANES), jnp.float32),
        ],
        name="output",
    )(value, starts, prefix, rates, residues, query, skip)


def summed_over_tp(value):
    pair = lax.ppermute(value, "tp", [(0, 1), (1, 0), (2, 3), (3, 2)])
    near = value + pair
    far = lax.ppermute(near, "tp", [(0, 2), (2, 0), (1, 3), (3, 1)])
    return jnp.stack([near, far])


def on_device(
    query_one,
    key_one,
    value_one,
    residual_in,
    medium_taps,
    skip_one,
    norm_gain,
    query_two,
    key_two,
    residues,
    decay_rates,
    skip_two,
):
    rows, channels = query_one.shape
    forward, backward = transform_tables(2 * HALF)
    tables = (
        jnp.asarray(np.concatenate(split_table(forward), axis=0)),
        jnp.asarray(np.concatenate(split_table(backward), axis=0)),
    )
    skip_row = skip_one[None, :]
    product_high = key_one[HALF:] * value_one[HALF:]
    count = lax.axis_size("ctx")
    before = lax.ppermute(product_high, "ctx", [(d, d + 1) for d in range(count - 1)])
    product_low = key_one[:HALF] * value_one[:HALF]
    high, square_high = medium_block(
        product_low, product_high, medium_taps, query_one, residual_in, skip_row, tables, 1
    )
    low, square_low = medium_block(
        before, product_low, medium_taps, query_one, residual_in, skip_row, tables, 0
    )
    residual_out = jnp.concatenate([low, high], axis=0)
    total_channels = channels * lax.axis_size("tp")
    value_two, ends, prefix = local_states(
        low,
        high,
        key_two,
        summed_over_tp(square_low),
        summed_over_tp(square_high),
        norm_gain[None, :],
        decay_rates,
        total_channels,
    )
    tiles = ends.shape[0] * ends.shape[1]
    here = lax.axis_index("ctx")
    rate_tile = lax.dynamic_slice(
        decay_rates,
        (SUB * (here // ends.shape[1]), LANES * (here % ends.shape[1])),
        (SUB, LANES),
    )
    gathered = lax.all_to_all(
        ends.reshape(tiles, SUB, LANES), "ctx", split_axis=0, concat_axis=0, tiled=True
    )
    starts = lax.all_to_all(
        scanned(rate_tile, gathered, rows), "ctx", split_axis=0, concat_axis=0, tiled=True
    ).reshape(ends.shape)
    result = long_output(
        value_two, starts, prefix, decay_rates, residues, query_two, skip_two[None, :]
    )
    return (residual_out, result)


def solution(mesh):
    in_specs = (
        P("ctx", "tp"),
        P("ctx", "tp"),
        P("ctx", "tp"),
        P("ctx", "tp"),
        P(None, "tp"),
        P("tp"),
        P("tp"),
        P("ctx", "tp"),
        P("ctx", "tp"),
        P(None, "tp"),
        P(None, "tp"),
        P("tp"),
    )
    out_specs = (P("ctx", "tp"), P("ctx", "tp"))
    return jax.shard_map(
        on_device, mesh=mesh, in_specs=in_specs, out_specs=out_specs, check_vma=False
    )
```

```python
import functools
import math

import jax
import jax.numpy as jnp
import numpy as np
from jax import lax
from jax.experimental import pallas as pl
from jax.experimental.pallas import tpu as pltpu
from jax.sharding import PartitionSpec as P

HALF = 128
LANES = 128
SUB = 8
STEPS = HALF // SUB
WIDE = 256


def split_table(table):
    upper = table.astype(jnp.bfloat16)
    lower = (table - upper.astype(np.float64)).astype(jnp.bfloat16)
    return upper, lower


def transform_tables(count):
    half = count // 2
    freq = np.arange(half)[:, None]
    time = np.arange(count)[None, :]
    angle = 2.0 * math.pi * ((freq * time) % count) / count
    even = np.cos(angle)
    odd = -np.sin(angle)
    odd[0] = np.where(np.arange(count) % 2 == 0, 1.0, -1.0)
    forward = np.concatenate([even, odd], axis=0)
    weight = np.full((half, 1), 2.0 / count)
    weight[0] = 1.0 / count
    backward = np.concatenate([even * weight, odd * weight], axis=0).T[half:]
    return forward, backward


def dot32(left, right):
    return jnp.dot(left, right, preferred_element_type=jnp.float32)


def on_chip(value):
    return pltpu.with_memory_space_constraint(value, pltpu.VMEM)


def local_call(kernel, name, out_shape, operands, scratch=()):
    call = pl.pallas_call(
        kernel,
        in_specs=[pl.BlockSpec(memory_space=pltpu.VMEM)] * len(operands),
        out_specs=jax.tree.map(lambda _: pl.BlockSpec(memory_space=pltpu.VMEM), out_shape),
        out_shape=jax.tree.map(lambda s: pltpu.VMEM(s.shape, s.dtype), out_shape),
        scratch_shapes=list(scratch),
        compiler_params=pltpu.CompilerParams(vmem_limit_bytes=8 << 20),
        name=name,
    )
    return call(*[on_chip(operand) for operand in operands])


def shape_of(shape, dtype):
    return jax.ShapeDtypeStruct(shape, dtype)


def tap_kernel(taps_ref, fwd_ref, even_ref, cross_ref, last_ref):
    count = 2 * HALF
    for start in range(0, taps_ref.shape[1], WIDE):
        cols = pl.ds(start, WIDE)
        both = dot32(fwd_ref[:, :HALF], taps_ref[:, cols])
        spec = both[:count] + both[count:]
        even, odd = spec[:HALF], spec[HALF:]
        first = lax.broadcasted_iota(jnp.int32, even.shape, 0) == 0
        even_ref[:, cols] = even
        cross_ref[:, cols] = jnp.where(first, 0.0, odd)
        last_ref[:, cols] = jnp.where(first, odd, even)


def filter_kernel(
    row_start,
    before_ref,
    here_ref,
    even_ref,
    cross_ref,
    last_ref,
    query_ref,
    resid_ref,
    skip_ref,
    fwd_ref,
    bwd_ref,
    out_ref,
    square_ref,
):
    count = 2 * HALF
    rows = pl.ds(row_start, HALF)
    total = None
    ahead = None
    starts = list(range(0, here_ref.shape[1], WIDE))
    for index in range(len(starts) + 1):
        spec = ahead
        if index < len(starts):
            cols = pl.ds(starts[index], WIDE)
            signal = jnp.concatenate([before_ref[:, cols], here_ref[:, cols]], axis=0)
            both = dot32(fwd_ref[...], signal)
            ahead = both[:count] + both[count:]
        if index == 0:
            continue
        cols = pl.ds(starts[index - 1], WIDE)
        sig_even, sig_odd = spec[:HALF], spec[HALF:]
        tap_cross = cross_ref[:, cols]
        joint = jnp.concatenate(
            [
                sig_even * even_ref[:, cols] - sig_odd * tap_cross,
                sig_even * tap_cross + sig_odd * last_ref[:, cols],
            ],
            axis=0,
        )
        joint_hi = joint.astype(jnp.bfloat16)
        joint_lo = (joint - joint_hi.astype(jnp.float32)).astype(jnp.bfloat16)
        back = dot32(bwd_ref[...], joint_hi)
        filtered = back[:HALF] + back[HALF:] + dot32(bwd_ref[:HALF], joint_lo)
        mixed = filtered + skip_ref[:, cols] * here_ref[:, cols].astype(jnp.float32)
        result = (
            resid_ref[rows, cols].astype(jnp.float32)
            + query_ref[rows, cols].astype(jnp.float32) * mixed
        ).astype(jnp.bfloat16)
        out_ref[:, cols] = result
        wide = result.astype(jnp.float32)
        squares = wide * wide
        for lane in range(0, WIDE, LANES):
            part = squares[:, lane : lane + LANES]
            total = part if total is None else total + part
    summed = jnp.sum(total.T, axis=0, keepdims=True)
    square_ref[...] = jnp.broadcast_to(summed, square_ref.shape)


def medium_block(before, here, spectrum, query, resid, skip, tables, row_start):
    return local_call(
        functools.partial(filter_kernel, row_start),
        "medium",
        [
            shape_of(here.shape, jnp.bfloat16),
            shape_of((SUB, HALF), jnp.float32),
        ],
        (before, here, *spectrum, query, resid, skip, *tables),
    )


def sublane_iota():
    return lax.broadcasted_iota(jnp.int32, (SUB, LANES), 0)


def row_of(ref, row, cols):
    return jnp.broadcast_to(ref[row : row + 1, cols], (SUB, LANES))


def lane_blocks(channels, body):
    def step(block, carry):
        body(block, pl.ds(pl.multiple_of(block * LANES, LANES), LANES))
        return carry

    lax.fori_loop(0, channels // LANES, step, 0)


def state_kernel(
    row_start,
    total_channels,
    with_later,
    *refs,
):
    part_ref, key_ref, near_ref, far_ref, gain_ref, rate_ref = refs[:6]
    later_ref = refs[6] if with_later else None
    value_ref, end_ref, state_ref = refs[6 + with_later : 9 + with_later]
    wide_ref, scale_ref = refs[9 + with_later :]
    modes = rate_ref.shape[0]
    blocks = end_ref.shape[0]
    rows = pl.ds(row_start, HALF)
    scale = lax.rsqrt((near_ref[...] + far_ref[...]) / total_channels + 1e-05)
    scale_ref[...] = jnp.broadcast_to(scale[:1], (HALF, HALF)).T

    def body(block, cols):
        value = (
            key_ref[rows, cols].astype(jnp.float32)
            * part_ref[:, cols].astype(jnp.float32)
            * scale_ref[...]
            * gain_ref[:, cols]
        ).astype(jnp.bfloat16)
        value_ref[:, cols] = value
        wide_ref[...] = value.astype(jnp.float32)
        rates = [row_of(rate_ref, m, cols) for m in range(modes)]
        decay = [jnp.exp(-rate) for rate in rates]
        held = [None] * modes
        for i in range(STEPS):
            step = wide_ref[pl.ds(i, SUB, stride=STEPS), :]
            for m in range(modes):
                held[m] = step if i == 0 else held[m] * decay[m] + step
        remaining = (sublane_iota() - (SUB - 1)).astype(jnp.float32) * float(STEPS)
        for m in range(modes):
            end_ref[block, m] = held[m]
            state = jnp.sum(held[m] * jnp.exp(rates[m] * remaining), axis=0, keepdims=True)
            if with_later:
                state = (
                    later_ref[m // SUB, block, m % SUB : m % SUB + 1, :]
                    + jnp.exp(-rates[m][:1] * float(HALF)) * state
                )
            state_ref[m // SUB, block, m % SUB : m % SUB + 1, :] = state

    lane_blocks(blocks * LANES, body)


def half_states(part, key, near, far, gain, rates, row_start, total_channels, later=None):
    channels = part.shape[1]
    modes = rates.shape[0]
    blocks = channels // LANES
    extra = () if later is None else (later,)
    return local_call(
        functools.partial(state_kernel, row_start, total_channels, len(extra)),
        "states",
        [
            shape_of(part.shape, jnp.bfloat16),
            shape_of((blocks, modes, SUB, LANES), jnp.float32),
            shape_of((modes // SUB, blocks, SUB, LANES), jnp.float32),
        ],
        (part, key, near, far, gain, rates, *extra),
        [pltpu.VMEM((HALF, LANES), jnp.float32), pltpu.VMEM((HALF, HALF), jnp.float32)],
    )


def scan_kernel(span, rate_ref, end_ref, start_ref):
    decay = jnp.exp(-rate_ref[...] * span)
    held = jnp.zeros_like(decay)
    for source in range(end_ref.shape[0]):
        start_ref[source] = held
        held = held * decay + end_ref[source]


def scanned(rate_tile, ends, span):
    return local_call(
        functools.partial(scan_kernel, float(span)),
        "scan",
        shape_of(ends.shape, ends.dtype),
        (rate_tile, ends),
    )


def short_kernel(low_ref, high_ref, rate_ref, residue_ref, near_ref, wide_ref, tap_ref):
    modes = rate_ref.shape[0]

    def body(block, cols):
        for start in range(0, STEPS, SUB):
            offset = (sublane_iota() + start).astype(jnp.float32)
            taps = None
            for m in range(modes):
                rate = row_of(rate_ref, m, cols)
                term = row_of(residue_ref, m, cols) * jnp.sqrt(rate) * jnp.exp(-rate * offset)
                taps = term if taps is None else taps + term
            tap_ref[start : start + SUB, :] = taps
        for half, value_ref in enumerate((low_ref, high_ref)):
            wide_ref[...] = value_ref[:, cols].astype(jnp.float32)
            steps = [wide_ref[pl.ds(i, SUB, stride=STEPS), :] for i in range(STEPS)]
            sums = [None] * STEPS
            for k in range(STEPS):
                tap = jnp.broadcast_to(tap_ref[k : k + 1, :], (SUB, LANES))
                for i in range(k, STEPS):
                    term = tap * steps[i - k]
                    sums[i] = term if k == 0 else sums[i] + term
            for i in range(STEPS):
                near_ref[half * STEPS + i, :, cols] = sums[i]

    lane_blocks(low_ref.shape[1], body)


def short_part(low, high, rates, residues):
    channels = low.shape[1]
    return local_call(
        short_kernel,
        "short",
        shape_of((2 * STEPS, SUB, channels), jnp.float32),
        (low, high, rates, residues),
        [pltpu.VMEM((HALF, LANES), jnp.float32), pltpu.VMEM((STEPS, LANES), jnp.float32)],
    )


def shifted_down(value, count):
    return jnp.where(sublane_iota() >= count, pltpu.roll(value, count, axis=0), 0.0)


def prefix_kernel(low_ref, high_ref, rate_ref, low_out_ref, high_out_ref):
    modes = rate_ref.shape[0]

    def body(block, cols):
        for m in range(modes):
            rate = row_of(rate_ref, m, cols)
            spans = [jnp.exp(rate * float(-STEPS * span)) for span in (1, 2, 4)]
            run = low_ref[block, m]
            for span, factor in zip((1, 2, 4), spans):
                run = run + factor * shifted_down(run, span)
            low_out_ref[block, m] = shifted_down(run, 1)
            carried = jnp.broadcast_to(run[SUB - 1 :], (SUB, LANES))
            run = high_ref[block, m]
            for span, factor in zip((1, 2, 4), spans):
                run = run + factor * shifted_down(run, span)
            position = sublane_iota().astype(jnp.float32) * float(-STEPS)
            high_out_ref[block, m] = shifted_down(run, 1) + jnp.exp(rate * position) * carried

    lane_blocks(low_ref.shape[0] * LANES, body)


def prefixes(low, high, rates):
    return local_call(
        prefix_kernel,
        "prefix",
        [shape_of(low.shape, low.dtype), shape_of(high.shape, high.dtype)],
        (low, high, rates),
    )


def output_kernel(
    low_ref,
    high_ref,
    near_ref,
    start_ref,
    low_prefix_ref,
    high_prefix_ref,
    rate_ref,
    residue_ref,
    query_ref,
    skip_ref,
    out_ref,
    mixed_ref,
):
    modes = rate_ref.shape[0]

    def body(block, cols):
        position = sublane_iota().astype(jnp.float32) * float(-STEPS) - 1.0
        for half, (value_ref, prefix_ref) in enumerate(
            ((low_ref, low_prefix_ref), (high_ref, high_prefix_ref))
        ):
            decay, held = [], []
            for m in range(modes):
                rate = row_of(rate_ref, m, cols)
                factor = row_of(residue_ref, m, cols) * jnp.sqrt(rate)
                start = jnp.broadcast_to(
                    start_ref[m // SUB, block, m % SUB : m % SUB + 1, :], (SUB, LANES)
                )
                one = jnp.exp(-rate)
                decay.append(one)
                reach = jnp.exp(rate * (position - float(half * HALF)))
                held.append(factor * (prefix_ref[block, m] * one + reach * start))
            for i in range(STEPS):
                if i > 0:
                    held = [h * d for h, d in zip(held, decay)]
                terms = held + [near_ref[half * STEPS + i, :, cols]]
                while len(terms) > 1:
                    odd = terms[len(terms) // 2 * 2 :]
                    terms = [a + b for a, b in zip(terms[::2], terms[1::2])] + odd
                mixed_ref[pl.ds(i, SUB, stride=STEPS), :] = terms[0]
            rows = pl.ds(half * HALF, HALF)
            out_ref[rows, cols] = (
                query_ref[rows, cols].astype(jnp.float32)
                * (mixed_ref[...] + skip_ref[:, cols] * value_ref[:, cols].astype(jnp.float32))
            ).astype(jnp.bfloat16)

    lane_blocks(query_ref.shape[1], body)


def long_output(low, high, near, starts, low_prefix, high_prefix, rates, residues, query, skip):
    return local_call(
        output_kernel,
        "output",
        shape_of(query.shape, jnp.bfloat16),
        (low, high, near, starts, low_prefix, high_prefix, rates, residues, query, skip),
        [pltpu.VMEM((HALF, LANES), jnp.float32)],
    )


def summed_over_tp(value):
    pair = lax.ppermute(value, "tp", [(0, 1), (1, 0), (2, 3), (3, 2)])
    near = value + pair
    far = lax.ppermute(near, "tp", [(0, 2), (2, 0), (1, 3), (3, 1)])
    return near, far


def on_device(
    query_one,
    key_one,
    value_one,
    residual_in,
    medium_taps,
    skip_one,
    norm_gain,
    query_two,
    key_two,
    residues,
    decay_rates,
    skip_two,
):
    rows, channels = query_one.shape
    forward, backward = transform_tables(2 * HALF)
    tables = (
        jnp.asarray(np.concatenate(split_table(forward), axis=0)),
        jnp.asarray(np.concatenate(split_table(backward), axis=0)),
    )
    skip_row = skip_one[None, :]
    gain_row = norm_gain[None, :]
    product_high = key_one[HALF:] * value_one[HALF:]
    count = lax.axis_size("ctx")
    before = lax.ppermute(product_high, "ctx", [(d, d + 1) for d in range(count - 1)])
    product_low = key_one[:HALF] * value_one[:HALF]
    spectrum = local_call(
        tap_kernel,
        "taps",
        [shape_of(medium_taps.shape, jnp.float32)] * 3,
        (medium_taps, tables[0]),
    )
    high, square_high = medium_block(
        product_low, product_high, spectrum, query_one, residual_in, skip_row, tables, HALF
    )
    sums_high = summed_over_tp(square_high)
    low, square_low = medium_block(
        before, product_low, spectrum, query_one, residual_in, skip_row, tables, 0
    )
    sums_low = summed_over_tp(square_low)
    total_channels = channels * lax.axis_size("tp")
    value_high, end_high, state_high = half_states(
        high, key_two, *sums_high, gain_row, decay_rates, HALF, total_channels
    )
    value_low, end_low, state = half_states(
        low, key_two, *sums_low, gain_row, decay_rates, 0, total_channels, state_high
    )
    tiles = state.shape[0] * state.shape[1]
    here = lax.axis_index("ctx")
    rate_tile = lax.dynamic_slice(
        decay_rates,
        (SUB * (here // state.shape[1]), LANES * (here % state.shape[1])),
        (SUB, LANES),
    )
    gathered = lax.all_to_all(
        state.reshape(tiles, SUB, LANES), "ctx", split_axis=0, concat_axis=0, tiled=True
    )
    near = short_part(value_low, value_high, decay_rates, residues)
    starts = lax.all_to_all(
        scanned(rate_tile, gathered, rows), "ctx", split_axis=0, concat_axis=0, tiled=True
    ).reshape(state.shape)
    low_prefix, high_prefix = prefixes(end_low, end_high, decay_rates)
    residual_out = jnp.concatenate([low, high], axis=0)
    result = long_output(
        value_low,
        value_high,
        near,
        starts,
        low_prefix,
        high_prefix,
        decay_rates,
        residues,
        query_two,
        skip_two[None, :],
    )
    return (residual_out, result)


def solution(mesh):
    in_specs = (
        P("ctx", "tp"),
        P("ctx", "tp"),
        P("ctx", "tp"),
        P("ctx", "tp"),
        P(None, "tp"),
        P("tp"),
        P("tp"),
        P("ctx", "tp"),
        P("ctx", "tp"),
        P(None, "tp"),
        P(None, "tp"),
        P("tp"),
    )
    out_specs = (P("ctx", "tp"), P("ctx", "tp"))
    return jax.shard_map(
        on_device, mesh=mesh, in_specs=in_specs, out_specs=out_specs, check_vma=False
    )
```

```python
import functools
import math

import jax
import jax.numpy as jnp
import numpy as np
from jax import lax
from jax.experimental import pallas as pl
from jax.experimental.pallas import tpu as pltpu
from jax.sharding import PartitionSpec as P

HALF = 128
LANES = 128
SUB = 8
STEPS = HALF // SUB
WIDE = 256
GROUP = 8


def split_table(table):
    upper = table.astype(jnp.bfloat16)
    lower = (table - upper.astype(np.float64)).astype(jnp.bfloat16)
    return upper, lower


def transform_tables(count):
    half = count // 2
    freq = np.arange(half)[:, None]
    time = np.arange(count)[None, :]
    angle = 2.0 * math.pi * ((freq * time) % count) / count
    even = np.cos(angle)
    odd = -np.sin(angle)
    odd[0] = np.where(np.arange(count) % 2 == 0, 1.0, -1.0)
    forward = np.concatenate([even, odd], axis=0)
    weight = np.full((half, 1), 2.0 / count)
    weight[0] = 1.0 / count
    backward = np.concatenate([even * weight, odd * weight], axis=0).T[half:]
    return forward, backward


def dot32(left, right):
    return jnp.dot(left, right, preferred_element_type=jnp.float32)


HBM = pltpu.HBM


def local_call(
    kernel, name, out_shape, operands, scratch=(), far_in=(), far_out=(), aliases={}
):
    outputs = out_shape if isinstance(out_shape, list) else [out_shape]
    near = pl.BlockSpec(memory_space=pltpu.VMEM)
    far = pl.BlockSpec(memory_space=HBM)
    call = pl.pallas_call(
        kernel,
        in_specs=[far if k in far_in else near for k in range(len(operands))],
        out_specs=[far if k in far_out else near for k in range(len(outputs))],
        out_shape=[
            (HBM if k in far_out else pltpu.VMEM)(o.shape, o.dtype) for k, o in enumerate(outputs)
        ],
        scratch_shapes=list(scratch),
        compiler_params=pltpu.CompilerParams(vmem_limit_bytes=8 << 20),
        input_output_aliases=aliases,
        name=name,
    )
    results = call(
        *[
            pltpu.with_memory_space_constraint(operand, HBM if k in far_in else pltpu.VMEM)
            for k, operand in enumerate(operands)
        ]
    )
    return results if isinstance(out_shape, list) else results[0]


def shape_of(shape, dtype):
    return jax.ShapeDtypeStruct(shape, dtype)


def forward_part(fwd, signal):
    count = 2 * HALF
    both = dot32(fwd, signal)
    return both[:count] + both[count:]


def filtered_result(spec, taps, here, skip, query, resid, bwd):
    even, cross, last = taps
    sig_even, sig_odd = spec[:HALF], spec[HALF:]
    joint = jnp.concatenate(
        [sig_even * even - sig_odd * cross, sig_even * cross + sig_odd * last], axis=0
    )
    joint_hi = joint.astype(jnp.bfloat16)
    joint_lo = (joint - joint_hi.astype(jnp.float32)).astype(jnp.bfloat16)
    back = dot32(bwd, joint_hi)
    filtered = back[:HALF] + back[HALF:] + dot32(bwd[:HALF], joint_lo)
    mixed = filtered + skip * here.astype(jnp.float32)
    return (resid.astype(jnp.float32) + query.astype(jnp.float32) * mixed).astype(jnp.bfloat16)


def squares_added(total, result):
    wide = result.astype(jnp.float32)
    squares = wide * wide
    for lane in range(0, WIDE, LANES):
        part = squares[:, lane : lane + LANES]
        total = part if total is None else total + part
    return total


def write_squares(total, square_ref):
    summed = jnp.sum(total.T, axis=0, keepdims=True)
    square_ref[...] = jnp.broadcast_to(summed, square_ref.shape)


def upper_kernel(
    here_ref,
    key_far,
    value_far,
    taps_far,
    fwd_far,
    bwd_far,
    query_far,
    resid_far,
    skip_far,
    out_ref,
    square_ref,
    before_ref,
    even_ref,
    cross_ref,
    last_ref,
    key_ref,
    value_ref,
    taps_ref,
    fwd_ref,
    bwd_ref,
    query_ref,
    resid_ref,
    skip_ref,
    sems,
):
    rows = pl.ds(HALF, HALF)
    first_rows = pl.ds(0, HALF)
    copies = [
        pltpu.make_async_copy(source, target, sems.at[k])
        for k, (source, target) in enumerate(
            (
                (fwd_far, fwd_ref),
                (taps_far, taps_ref),
                (key_far.at[first_rows, :], key_ref),
                (value_far.at[first_rows, :], value_ref),
                (bwd_far, bwd_ref),
                (query_far.at[rows, :], query_ref),
                (resid_far.at[rows, :], resid_ref),
                (skip_far, skip_ref),
            )
        )
    ]
    for copy in copies:
        copy.start()
    total = None
    starts = list(range(0, here_ref.shape[1], WIDE))
    specs = {}
    for index in range(len(starts) + 2):
        if index < len(starts):
            cols = pl.ds(starts[index], WIDE)
            if index == 0:
                copies[0].wait()
                copies[1].wait()
            spec = forward_part(fwd_ref[:, :HALF], taps_ref[:, cols])
            even, odd = spec[:HALF], spec[HALF:]
            first = lax.broadcasted_iota(jnp.int32, even.shape, 0) == 0
            even_ref[:, cols] = even
            cross_ref[:, cols] = jnp.where(first, 0.0, odd)
            last_ref[:, cols] = jnp.where(first, odd, even)
        if 1 <= index <= len(starts):
            cols = pl.ds(starts[index - 1], WIDE)
            if index == 1:
                copies[2].wait()
                copies[3].wait()
            before = (
                key_ref[:, cols].astype(jnp.float32) * value_ref[:, cols].astype(jnp.float32)
            ).astype(jnp.bfloat16)
            before_ref[:, cols] = before
            signal = jnp.concatenate([before, here_ref[:, cols]], axis=0)
            specs[index - 1] = forward_part(fwd_ref[...], signal)
        if index >= 2:
            cols = pl.ds(starts[index - 2], WIDE)
            if index == 2:
                for copy in copies[4:]:
                    copy.wait()
            result = filtered_result(
                specs.pop(index - 2),
                (even_ref[:, cols], cross_ref[:, cols], last_ref[:, cols]),
                here_ref[:, cols],
                skip_ref[:, cols],
                query_ref[:, cols],
                resid_ref[:, cols],
                bwd_ref[...],
            )
            out_ref[:, cols] = result
            total = squares_added(total, result)
    write_squares(total, square_ref)


def upper_block(here, key, value, taps, tables, query, resid, skip):
    half = shape_of(here.shape, jnp.bfloat16)
    spectrum = shape_of(taps.shape, jnp.float32)
    return local_call(
        upper_kernel,
        "upper",
        [half, shape_of((SUB, HALF), jnp.float32), half, spectrum, spectrum, spectrum],
        (here, key, value, taps, *tables, query, resid, skip),
        [
            pltpu.VMEM(here.shape, jnp.bfloat16),
            pltpu.VMEM(here.shape, jnp.bfloat16),
            pltpu.VMEM(taps.shape, jnp.bfloat16),
            pltpu.VMEM(tables[0].shape, jnp.bfloat16),
            pltpu.VMEM(tables[1].shape, jnp.bfloat16),
            pltpu.VMEM(here.shape, jnp.bfloat16),
            pltpu.VMEM(here.shape, jnp.bfloat16),
            pltpu.VMEM(skip.shape, jnp.float32),
            pltpu.SemaphoreType.DMA((8,)),
        ],
        far_in=tuple(range(1, 9)),
    )


def lower_kernel(
    before_ref,
    here_ref,
    even_ref,
    cross_ref,
    last_ref,
    query_ref,
    resid_ref,
    skip_ref,
    fwd_ref,
    bwd_ref,
    out_ref,
    square_ref,
):
    rows = pl.ds(0, HALF)
    total = None
    spec = None
    starts = list(range(0, here_ref.shape[1], WIDE))
    for index in range(len(starts) + 1):
        ready = spec
        if index < len(starts):
            cols = pl.ds(starts[index], WIDE)
            signal = jnp.concatenate([before_ref[:, cols], here_ref[:, cols]], axis=0)
            spec = forward_part(fwd_ref[...], signal)
        if index > 0:
            cols = pl.ds(starts[index - 1], WIDE)
            result = filtered_result(
                ready,
                (even_ref[:, cols], cross_ref[:, cols], last_ref[:, cols]),
                here_ref[:, cols],
                skip_ref[:, cols],
                query_ref[rows, cols],
                resid_ref[rows, cols],
                bwd_ref[...],
            )
            out_ref[:, cols] = result
            total = squares_added(total, result)
    write_squares(total, square_ref)


def lower_block(before, here, spectrum, query, resid, skip, tables):
    return local_call(
        lower_kernel,
        "lower",
        [shape_of(here.shape, jnp.bfloat16), shape_of((SUB, HALF), jnp.float32)],
        (before, here, *spectrum, query, resid, skip, *tables),
    )


def sublane_iota():
    return lax.broadcasted_iota(jnp.int32, (SUB, LANES), 0)


def row_of(ref, row, cols):
    return jnp.broadcast_to(ref[row : row + 1, cols], (SUB, LANES))


def lane_blocks(channels, body):
    def step(pair, carry):
        for side in range(2):
            block = pair * 2 + side
            body(block, column(block), side)
        return carry

    lax.fori_loop(0, channels // (2 * LANES), step, 0)


def column(block):
    return pl.ds(pl.multiple_of(block * LANES, LANES), LANES)


def state_kernel(row_start, total_channels, last, *refs):
    part_ref, key_ref, near_ref, far_ref, gain_ref, rate_ref = refs[:6]
    if last:
        later_ref = refs[6]
        refs = refs[2:]
    value_ref, end_ref, state_ref, joined_ref, wide_ref, scale_ref, decay_ref, sems = refs[6:14]
    held_ref = end_ref if last else refs[14]
    join = pltpu.make_async_copy(
        part_ref, joined_ref.at[pl.ds(row_start, HALF), :], sems.at[0]
    )
    join.start()
    modes = rate_ref.shape[0]
    blocks = end_ref.shape[0]
    rows = pl.ds(row_start, HALF)
    scale = lax.rsqrt((near_ref[...] + far_ref[...]) / total_channels + 1e-05)
    scale_ref[...] = jnp.broadcast_to(scale[:1], (HALF, HALF)).T

    def body(block, cols, side):
        decay_ref[side] = jnp.exp(-rate_ref[:, cols])
        value = (
            key_ref[rows, cols].astype(jnp.float32)
            * part_ref[:, cols].astype(jnp.float32)
            * scale_ref[...]
            * gain_ref[:, cols]
        ).astype(jnp.bfloat16)
        value_ref[:, cols] = value
        wide_ref[side] = value.astype(jnp.float32)
        every = pl.ds(0, LANES)
        decay = [row_of(decay_ref.at[side], m, every) for m in range(modes)]
        held = [None] * modes
        for i in range(STEPS):
            step = wide_ref[side, pl.ds(i, SUB, stride=STEPS), :]
            for m in range(modes):
                held[m] = step if i == 0 else held[m] * decay[m] + step
        remaining = (sublane_iota() - (SUB - 1)).astype(jnp.float32) * float(STEPS)
        for m in range(modes):
            held_ref[block, m] = held[m]
        if not last:
            pltpu.make_async_copy(held_ref.at[block], end_ref.at[block], sems.at[1]).start()
        tiles = []
        for group in range(modes // SUB):
            span = range(group * SUB, (group + 1) * SUB)
            state = gathered_sums(
                [held[m] * jnp.exp(row_of(rate_ref, m, cols) * remaining) for m in span]
            )
            if last:
                rate = rate_ref[group * SUB : (group + 1) * SUB, cols]
                state = later_ref[group, block] + jnp.exp(-rate * float(HALF)) * state
            tiles.append(state)
        if last:
            joint = jnp.concatenate(tiles, axis=0).astype(jnp.bfloat16)
            for member in range(GROUP):
                state_ref[member, :, cols] = joint
        else:
            for group, state in enumerate(tiles):
                state_ref[group, block] = state

    lane_blocks(blocks * LANES, body)
    join.wait()
    if not last:
        pltpu.make_async_copy(held_ref, end_ref, sems.at[1]).wait()


def gathered_sums(values):
    row = sublane_iota()
    span = 1
    while span < SUB:
        upper = (row & span) != 0
        values = [
            jnp.where(upper, b, a) + pltpu.roll(jnp.where(upper, a, b), span, axis=0)
            for a, b in zip(values[::2], values[1::2])
        ]
        span *= 2
    return values[0]


def half_states(part, key, near, far, gain, rates, row_start, total_channels, last=()):
    channels = part.shape[1]
    modes = rates.shape[0]
    blocks = channels // LANES
    ends = (blocks, modes, SUB, LANES)
    joined = shape_of((2 * HALF, channels), jnp.bfloat16)
    scratch = [
        pltpu.VMEM((2, HALF, LANES), jnp.float32),
        pltpu.VMEM((HALF, HALF), jnp.float32),
        pltpu.VMEM((2, modes, LANES), jnp.float32),
        pltpu.SemaphoreType.DMA((2,)),
    ]
    if not last:
        scratch += [pltpu.VMEM(ends, jnp.float32)]
    return local_call(
        functools.partial(state_kernel, row_start, total_channels, len(last)),
        "states",
        [
            shape_of(part.shape, jnp.bfloat16),
            shape_of(ends, jnp.float32),
            shape_of((GROUP, modes, channels), jnp.bfloat16)
            if last
            else shape_of((modes // SUB, blocks, SUB, LANES), jnp.float32),
            joined,
        ],
        (part, key, near, far, gain, rates, *last),
        scratch,
        far_in=(7,) if last else (),
        far_out=(3,) if last else (1, 3),
        aliases={7: 3} if last else {},
    )


def member_index():
    return lax.rem(lax.axis_index("ctx"), GROUP)


def group_kernel(span, rate_ref, state_ref, total_ref, before_ref):
    member = member_index()

    def body(block, cols, side):
        decay = jnp.exp(rate_ref[:, cols] * -span)
        held = jnp.zeros_like(decay)
        before = held
        for source in range(GROUP):
            if source > 0:
                before = jnp.where(member == source, held, before)
            held = held * decay + state_ref[source, :, cols].astype(jnp.float32)
        total_ref[:, cols] = held.astype(jnp.bfloat16)
        before_ref[:, cols] = before

    lane_blocks(rate_ref.shape[1], body)


def group_scan(rates, states, span):
    return local_call(
        functools.partial(group_kernel, float(span)),
        "group",
        [shape_of(rates.shape, jnp.bfloat16), shape_of(rates.shape, jnp.float32)],
        (rates, states),
    )


def shifted_down(value, count):
    return jnp.where(sublane_iota() >= count, pltpu.roll(value, count, axis=0), 0.0)


def tree_sum(terms):
    while len(terms) > 1:
        odd = terms[len(terms) // 2 * 2 :]
        terms = [a + b for a, b in zip(terms[::2], terms[1::2])] + odd
    return terms[0]


def short_kernel(
    low_ref, high_ref, rate_ref, residue_ref, skip_ref, near_ref, wide_ref, tap_ref, made_ref, sem
):
    modes = rate_ref.shape[0]

    def body(block, cols, side):
        for start in range(0, STEPS, SUB):
            offset = (sublane_iota() + start).astype(jnp.float32)
            terms = []
            for m in range(modes):
                rate = row_of(rate_ref, m, cols)
                factor = row_of(residue_ref, m, cols) * jnp.sqrt(rate)
                terms.append(factor * jnp.exp(-rate * offset))
            tap_ref[side, start : start + SUB, :] = tree_sum(terms)
        for half, value_ref in enumerate((low_ref, high_ref)):
            wide_ref[side, half] = value_ref[:, cols].astype(jnp.float32)
            steps = [wide_ref[side, half, pl.ds(i, SUB, stride=STEPS), :] for i in range(STEPS)]
            skip = jnp.broadcast_to(skip_ref[:, cols], (SUB, LANES))
            sums = [None] * STEPS
            for k in range(STEPS):
                tap = jnp.broadcast_to(tap_ref[side, k : k + 1, :], (SUB, LANES))
                if k == 0:
                    tap = tap + skip
                for i in range(k, STEPS):
                    term = tap * steps[i - k]
                    sums[i] = term if k == 0 else sums[i] + term
            for i in range(STEPS):
                made_ref[block, pl.ds((half * STEPS + i) * SUB, SUB), :] = sums[i]
        pltpu.make_async_copy(made_ref.at[block], near_ref.at[block], sem).start()

    lane_blocks(low_ref.shape[1], body)
    pltpu.make_async_copy(made_ref, near_ref, sem).wait()


def short_part(low, high, rates, residues, skip):
    shape = (low.shape[1] // LANES, 2 * HALF, LANES)
    return local_call(
        short_kernel,
        "short",
        shape_of(shape, jnp.float32),
        (low, high, rates, residues, skip),
        [
            pltpu.VMEM((2, 2, HALF, LANES), jnp.float32),
            pltpu.VMEM((2, STEPS, LANES), jnp.float32),
            pltpu.VMEM(shape, jnp.float32),
            pltpu.SemaphoreType.DMA(()),
        ],
        far_out=(0,),
    )


def weights_of(residue_ref, rate_ref):
    rates = rate_ref[...]
    return residue_ref[...] * jnp.sqrt(rates) * jnp.exp(-rates)


def prefix_kernel(
    low_ref, far_high_ref, rate_ref, residue_ref, out_ref, weight_ref, high_ref, sems
):
    modes = rate_ref.shape[0]
    blocks = low_ref.shape[0]

    def arriving(block):
        return pltpu.make_async_copy(far_high_ref.at[block], high_ref.at[block], sems.at[block])

    for block in range(blocks):
        arriving(block).start()
    weight_ref[...] = weights_of(residue_ref, rate_ref)

    def body(block, cols, side):
        arriving(block).wait()
        for m in range(modes):
            rate = row_of(rate_ref, m, cols)
            weight = row_of(weight_ref, m, cols)
            spans = [jnp.exp(rate * float(-STEPS * span)) for span in (1, 2, 4)]
            run = low_ref[block, m]
            for span, factor in zip((1, 2, 4), spans):
                run = run + factor * shifted_down(run, span)
            out_ref[block, 0, m] = shifted_down(run, 1) * weight
            carried = jnp.broadcast_to(run[SUB - 1 :], (SUB, LANES))
            run = high_ref[block, m]
            for span, factor in zip((1, 2, 4), spans):
                run = run + factor * shifted_down(run, span)
            position = sublane_iota().astype(jnp.float32) * float(-STEPS)
            out_ref[block, 1, m] = (
                shifted_down(run, 1) + jnp.exp(rate * position) * carried
            ) * weight

    lane_blocks(blocks * LANES, body)


def prefixes(low, high, rates, residues):
    blocks, modes = low.shape[:2]
    return local_call(
        prefix_kernel,
        "prefix",
        shape_of((blocks, 2, modes, SUB, LANES), low.dtype),
        (low, high, rates, residues),
        [
            pltpu.VMEM(rates.shape, rates.dtype),
            pltpu.VMEM(high.shape, high.dtype),
            pltpu.SemaphoreType.DMA((blocks,)),
        ],
        far_in=(1,),
    )


def output_kernel(
    lag,
    near_ref,
    prefix_ref,
    before_ref,
    one_ref,
    two_ref,
    three_ref,
    rate_ref,
    residue_ref,
    query_ref,
    out_ref,
    mixed_ref,
    ready_ref,
    nears_ref,
    queries_ref,
    gain_ref,
    decay_ref,
    weight_ref,
    sems,
    out_sem,
):
    modes = rate_ref.shape[0]
    blocks = near_ref.shape[0]

    def arriving(block):
        return (
            pltpu.make_async_copy(near_ref.at[block], nears_ref.at[block], sems.at[0, block]),
            pltpu.make_async_copy(
                query_ref.at[:, column(block)], queries_ref.at[block], sems.at[1, block]
            ),
        )

    for block in range(blocks):
        for copy in arriving(block):
            copy.start()
    decay_ref[...] = jnp.exp(-rate_ref[...])
    rates = rate_ref[...]
    member = member_index().astype(jnp.float32)
    span = float(2 * HALF)
    level = jnp.exp(rates * (-span * GROUP))
    earlier = one_ref[...].astype(jnp.float32) + level * (
        two_ref[...].astype(jnp.float32) + level * three_ref[...].astype(jnp.float32)
    )
    start = before_ref[...] + jnp.exp(rates * (-span * member)) * earlier
    weight_ref[...] = weights_of(residue_ref, rate_ref) * start

    def corrected(block, side):
        cols = column(block)
        every = pl.ds(0, LANES)
        for group in range(modes // SUB):
            span = slice(group * SUB, (group + 1) * SUB)
            gain = weight_ref[span, cols]
            gain_ref[side, 0, span, :] = gain
            gain_ref[side, 1, span, :] = gain * jnp.exp(rate_ref[span, cols] * float(-HALF))
        position = sublane_iota().astype(jnp.float32) * float(-STEPS)
        decay = [row_of(decay_ref, m, cols) for m in range(modes)]
        held = [[], []]
        for m in range(modes):
            reach = jnp.exp(row_of(rate_ref, m, cols) * position)
            for half in range(2):
                gain = row_of(gain_ref.at[side, half], m, every)
                held[half].append(prefix_ref[block, half, m] + reach * gain)
        for i in range(STEPS):
            for half in range(2):
                if i > 0:
                    held[half] = [h * d for h, d in zip(held[half], decay)]
                mixed_ref[block, pl.ds((half * STEPS + i) * SUB, SUB), :] = tree_sum(held[half])

    def finished(block):
        cols = column(block)
        for copy in arriving(block):
            copy.wait()
        nears_ref[block] = nears_ref[block] + mixed_ref[block]
        for half in range(2):
            for s in range(SUB):
                rows = pl.ds(half * HALF + s * STEPS, STEPS)
                mixed = nears_ref[block, pl.ds(half * HALF + s, STEPS, stride=SUB), :]
                ready_ref[rows, cols] = (
                    queries_ref[block, rows, :].astype(jnp.float32) * mixed
                ).astype(jnp.bfloat16)
        pltpu.make_async_copy(ready_ref.at[:, cols], out_ref.at[:, cols], out_sem).start()

    for block in range(lag):
        corrected(block, block % 2)

    def step(pair, carry):
        for side in range(2):
            block = lag + pair * 2 + side
            finished(block - lag)
            corrected(block, side)
        return carry

    lax.fori_loop(0, (blocks - lag) // 2, step, 0)
    for block in range(blocks - lag, blocks):
        finished(block)
    pltpu.make_async_copy(ready_ref, out_ref, out_sem).wait()


def long_output(near, prefix, before, earlier, rates, residues, query):
    blocks = near.shape[0]
    return local_call(
        functools.partial(output_kernel, 2),
        "output",
        shape_of(query.shape, jnp.bfloat16),
        (near, prefix, before, *earlier, rates, residues, query),
        [
            pltpu.VMEM(near.shape, jnp.float32),
            pltpu.VMEM(query.shape, jnp.bfloat16),
            pltpu.VMEM(near.shape, jnp.float32),
            pltpu.VMEM((blocks, 2 * HALF, LANES), jnp.bfloat16),
            pltpu.VMEM((2, 2, *rates.shape[:1], LANES), jnp.float32),
            pltpu.VMEM(rates.shape, jnp.float32),
            pltpu.VMEM(rates.shape, jnp.float32),
            pltpu.SemaphoreType.DMA((2, blocks)),
            pltpu.SemaphoreType.DMA(()),
        ],
        far_in=(0, 8),
        far_out=(0,),
    )


def summed_with_pair(value):
    return value + lax.ppermute(value, "tp", [(0, 1), (1, 0), (2, 3), (3, 2)])


def across_pairs(value):
    return lax.ppermute(value, "tp", [(0, 2), (2, 0), (1, 3), (3, 1)])


def on_device(
    query_one,
    key_one,
    value_one,
    residual_in,
    medium_taps,
    skip_one,
    norm_gain,
    query_two,
    key_two,
    residues,
    decay_rates,
    skip_two,
):
    rows, channels = query_one.shape
    forward, backward = transform_tables(2 * HALF)
    tables = (
        jnp.asarray(np.concatenate(split_table(forward), axis=0)),
        jnp.asarray(np.concatenate(split_table(backward), axis=0)),
    )
    skip_row = skip_one[None, :]
    gain_row = norm_gain[None, :]
    skip_long = skip_two[None, :]
    product_high = key_one[HALF:] * value_one[HALF:]
    count = lax.axis_size("ctx")
    before = lax.ppermute(product_high, "ctx", [(d, d + 1) for d in range(count - 1)])
    high, square_high, product_low, *spectrum = upper_block(
        product_high, key_one, value_one, medium_taps, tables, query_one, residual_in, skip_row
    )
    near_high = summed_with_pair(square_high)
    far_high = across_pairs(near_high)
    total_channels = channels * lax.axis_size("tp")
    value_high, end_high, state_high, residual_out = half_states(
        high, key_two, near_high, far_high, gain_row, decay_rates, HALF, total_channels
    )
    before, state_high = lax.optimization_barrier((before, state_high))
    low, square_low = lower_block(
        before, product_low, spectrum, query_one, residual_in, skip_row, tables
    )
    near_low = summed_with_pair(square_low)
    far_low = across_pairs(near_low)
    value_low, end_low, state, residual_out = half_states(
        low,
        key_two,
        near_low,
        far_low,
        gain_row,
        decay_rates,
        0,
        total_channels,
        (state_high, residual_out),
    )
    members = [
        [first + k for k in range(GROUP)] for first in range(0, lax.axis_size("ctx"), GROUP)
    ]
    gathered = lax.all_to_all(
        state, "ctx", split_axis=0, concat_axis=0, tiled=True, axis_index_groups=members
    )
    near = short_part(value_low, value_high, decay_rates, residues, skip_long)
    prefix = prefixes(end_low, end_high, decay_rates, residues)
    gathered, near, prefix = lax.optimization_barrier((gathered, near, prefix))
    total, before_here = group_scan(decay_rates, gathered, rows)
    earlier = [
        lax.ppermute(total, "ctx", [(d, d + far) for d in range(count - far)])
        for far in range(GROUP, count, GROUP)
    ]
    result = long_output(
        near, prefix, before_here, earlier, decay_rates, residues, query_two
    )
    return (residual_out, result)


def solution(mesh):
    in_specs = (
        P("ctx", "tp"),
        P("ctx", "tp"),
        P("ctx", "tp"),
        P("ctx", "tp"),
        P(None, "tp"),
        P("tp"),
        P("tp"),
        P("ctx", "tp"),
        P("ctx", "tp"),
        P(None, "tp"),
        P(None, "tp"),
        P("tp"),
    )
    out_specs = (P("ctx", "tp"), P("ctx", "tp"))
    return jax.shard_map(
        on_device, mesh=mesh, in_specs=in_specs, out_specs=out_specs, check_vma=False
    )
```

```python
import functools
import math

import jax
import jax.numpy as jnp
import numpy as np
from jax import lax
from jax.experimental import pallas as pl
from jax.experimental.pallas import tpu as pltpu
from jax.sharding import PartitionSpec as P

HALF = 128
LANES = 128
SUB = 8
STEPS = HALF // SUB
WIDE = 256
GROUP = 8


def split_table(table):
    upper = table.astype(jnp.bfloat16)
    lower = (table - upper.astype(np.float64)).astype(jnp.bfloat16)
    return upper, lower


def transform_tables(count):
    half = count // 2
    freq = np.arange(half)[:, None]
    time = np.arange(count)[None, :]
    angle = 2.0 * math.pi * ((freq * time) % count) / count
    even = np.cos(angle)
    odd = -np.sin(angle)
    odd[0] = np.where(np.arange(count) % 2 == 0, 1.0, -1.0)
    forward = np.concatenate([even, odd], axis=0)
    weight = np.full((half, 1), 2.0 / count)
    weight[0] = 1.0 / count
    backward = np.concatenate([even * weight, odd * weight], axis=0).T[half:]
    return forward, backward


def dot32(left, right):
    return jnp.dot(left, right, preferred_element_type=jnp.float32)


HBM = pltpu.HBM


def local_call(
    kernel, name, out_shape, operands, scratch=(), far_in=(), far_out=(), aliases={}
):
    outputs = out_shape if isinstance(out_shape, list) else [out_shape]
    near = pl.BlockSpec(memory_space=pltpu.VMEM)
    far = pl.BlockSpec(memory_space=HBM)
    call = pl.pallas_call(
        kernel,
        in_specs=[far if k in far_in else near for k in range(len(operands))],
        out_specs=[far if k in far_out else near for k in range(len(outputs))],
        out_shape=[
            (HBM if k in far_out else pltpu.VMEM)(o.shape, o.dtype) for k, o in enumerate(outputs)
        ],
        scratch_shapes=list(scratch),
        compiler_params=pltpu.CompilerParams(vmem_limit_bytes=8 << 20),
        input_output_aliases=aliases,
        name=name,
    )
    results = call(
        *[
            pltpu.with_memory_space_constraint(operand, HBM if k in far_in else pltpu.VMEM)
            for k, operand in enumerate(operands)
        ]
    )
    return results if isinstance(out_shape, list) else results[0]


def shape_of(shape, dtype):
    return jax.ShapeDtypeStruct(shape, dtype)


def forward_part(fwd, signal):
    count = 2 * HALF
    both = dot32(fwd, signal)
    return both[:count] + both[count:]


def filtered_result(spec, taps, here, skip, query, resid, bwd):
    even, cross, last = taps
    sig_even, sig_odd = spec[:HALF], spec[HALF:]
    joint = jnp.concatenate(
        [sig_even * even - sig_odd * cross, sig_even * cross + sig_odd * last], axis=0
    )
    joint_hi = joint.astype(jnp.bfloat16)
    joint_lo = (joint - joint_hi.astype(jnp.float32)).astype(jnp.bfloat16)
    back = dot32(bwd, joint_hi)
    filtered = back[:HALF] + back[HALF:] + dot32(bwd[:HALF], joint_lo)
    mixed = filtered + skip * here.astype(jnp.float32)
    return (resid.astype(jnp.float32) + query.astype(jnp.float32) * mixed).astype(jnp.bfloat16)


def squares_added(total, result):
    wide = result.astype(jnp.float32)
    squares = wide * wide
    for lane in range(0, WIDE, LANES):
        part = squares[:, lane : lane + LANES]
        total = part if total is None else total + part
    return total


def write_squares(total, square_ref):
    summed = jnp.sum(total.T, axis=0, keepdims=True)
    square_ref[...] = jnp.broadcast_to(summed, square_ref.shape)


def upper_kernel(
    here_ref,
    key_far,
    value_far,
    taps_far,
    fwd_far,
    bwd_far,
    query_far,
    resid_far,
    skip_far,
    out_ref,
    square_ref,
    before_ref,
    even_ref,
    cross_ref,
    last_ref,
    key_ref,
    value_ref,
    taps_ref,
    fwd_ref,
    bwd_ref,
    query_ref,
    resid_ref,
    skip_ref,
    sems,
):
    rows = pl.ds(HALF, HALF)
    first_rows = pl.ds(0, HALF)
    copies = [
        pltpu.make_async_copy(source, target, sems.at[k])
        for k, (source, target) in enumerate(
            (
                (fwd_far, fwd_ref),
                (taps_far, taps_ref),
                (key_far.at[first_rows, :], key_ref),
                (value_far.at[first_rows, :], value_ref),
                (bwd_far, bwd_ref),
                (query_far.at[rows, :], query_ref),
                (resid_far.at[rows, :], resid_ref),
                (skip_far, skip_ref),
            )
        )
    ]
    for copy in copies:
        copy.start()
    total = None
    starts = list(range(0, here_ref.shape[1], WIDE))
    specs = {}
    for index in range(len(starts) + 2):
        if index < len(starts):
            cols = pl.ds(starts[index], WIDE)
            if index == 0:
                copies[0].wait()
                copies[1].wait()
            spec = forward_part(fwd_ref[:, :HALF], taps_ref[:, cols])
            even, odd = spec[:HALF], spec[HALF:]
            first = lax.broadcasted_iota(jnp.int32, even.shape, 0) == 0
            even_ref[:, cols] = even
            cross_ref[:, cols] = jnp.where(first, 0.0, odd)
            last_ref[:, cols] = jnp.where(first, odd, even)
        if 1 <= index <= len(starts):
            cols = pl.ds(starts[index - 1], WIDE)
            if index == 1:
                copies[2].wait()
                copies[3].wait()
            before = (
                key_ref[:, cols].astype(jnp.float32) * value_ref[:, cols].astype(jnp.float32)
            ).astype(jnp.bfloat16)
            before_ref[:, cols] = before
            signal = jnp.concatenate([before, here_ref[:, cols]], axis=0)
            specs[index - 1] = forward_part(fwd_ref[...], signal)
        if index >= 2:
            cols = pl.ds(starts[index - 2], WIDE)
            if index == 2:
                for copy in copies[4:]:
                    copy.wait()
            result = filtered_result(
                specs.pop(index - 2),
                (even_ref[:, cols], cross_ref[:, cols], last_ref[:, cols]),
                here_ref[:, cols],
                skip_ref[:, cols],
                query_ref[:, cols],
                resid_ref[:, cols],
                bwd_ref[...],
            )
            out_ref[:, cols] = result
            total = squares_added(total, result)
    write_squares(total, square_ref)


def upper_block(here, key, value, taps, tables, query, resid, skip):
    half = shape_of(here.shape, jnp.bfloat16)
    spectrum = shape_of(taps.shape, jnp.float32)
    return local_call(
        upper_kernel,
        "upper",
        [half, shape_of((SUB, HALF), jnp.float32), half, spectrum, spectrum, spectrum],
        (here, key, value, taps, *tables, query, resid, skip),
        [
            pltpu.VMEM(here.shape, jnp.bfloat16),
            pltpu.VMEM(here.shape, jnp.bfloat16),
            pltpu.VMEM(taps.shape, jnp.bfloat16),
            pltpu.VMEM(tables[0].shape, jnp.bfloat16),
            pltpu.VMEM(tables[1].shape, jnp.bfloat16),
            pltpu.VMEM(here.shape, jnp.bfloat16),
            pltpu.VMEM(here.shape, jnp.bfloat16),
            pltpu.VMEM(skip.shape, jnp.float32),
            pltpu.SemaphoreType.DMA((8,)),
        ],
        far_in=tuple(range(1, 9)),
    )


def lower_kernel(
    before_ref,
    here_ref,
    even_ref,
    cross_ref,
    last_ref,
    query_ref,
    resid_ref,
    skip_ref,
    fwd_ref,
    bwd_ref,
    out_ref,
    square_ref,
):
    rows = pl.ds(0, HALF)
    total = None
    spec = None
    starts = list(range(0, here_ref.shape[1], WIDE))
    for index in range(len(starts) + 1):
        ready = spec
        if index < len(starts):
            cols = pl.ds(starts[index], WIDE)
            signal = jnp.concatenate([before_ref[:, cols], here_ref[:, cols]], axis=0)
            spec = forward_part(fwd_ref[...], signal)
        if index > 0:
            cols = pl.ds(starts[index - 1], WIDE)
            result = filtered_result(
                ready,
                (even_ref[:, cols], cross_ref[:, cols], last_ref[:, cols]),
                here_ref[:, cols],
                skip_ref[:, cols],
                query_ref[rows, cols],
                resid_ref[rows, cols],
                bwd_ref[...],
            )
            out_ref[:, cols] = result
            total = squares_added(total, result)
    write_squares(total, square_ref)


def lower_block(before, here, spectrum, query, resid, skip, tables):
    return local_call(
        lower_kernel,
        "lower",
        [shape_of(here.shape, jnp.bfloat16), shape_of((SUB, HALF), jnp.float32)],
        (before, here, *spectrum, query, resid, skip, *tables),
    )


def sublane_iota():
    return lax.broadcasted_iota(jnp.int32, (SUB, LANES), 0)


def row_of(ref, row, cols):
    return jnp.broadcast_to(ref[row : row + 1, cols], (SUB, LANES))


def lane_blocks(channels, body):
    def step(pair, carry):
        for side in range(2):
            block = pair * 2 + side
            body(block, column(block), side)
        return carry

    lax.fori_loop(0, channels // (2 * LANES), step, 0)


def column(block):
    return pl.ds(pl.multiple_of(block * LANES, LANES), LANES)


def swept(wide_ref, decay_ref):
    decay = [row_of(decay_ref, m, pl.ds(0, LANES)) for m in range(decay_ref.shape[0])]
    held = None
    for i in range(STEPS):
        step = wide_ref[pl.ds(i, SUB, stride=STEPS), :]
        held = [step] * len(decay) if i == 0 else [h * d + step for h, d in zip(held, decay)]
    return held


def state_kernel(row_start, total_channels, last, *refs):
    part_ref, key_ref, near_ref, far_ref, gain_ref, rate_ref = refs[:6]
    if last:
        later_ref = refs[6]
        value_ref, state_ref, joined_ref, wide_ref, scale_ref, decay_ref, sems = refs[8:]
        made_ref = value_ref
    else:
        value_ref, state_ref, joined_ref, end_ref = refs[6:10]
        wide_ref, scale_ref, decay_ref, sems, made_ref, held_ref = refs[10:]
    join = pltpu.make_async_copy(
        part_ref, joined_ref.at[pl.ds(row_start, HALF), :], sems.at[0]
    )
    join.start()
    modes, channels = rate_ref.shape
    rows = pl.ds(row_start, HALF)
    scale = lax.rsqrt((near_ref[...] + far_ref[...]) / total_channels + 1e-05)
    scale_ref[...] = jnp.broadcast_to(scale[:1], (HALF, HALF)).T

    def body(block, cols, side):
        decay_ref[side] = jnp.exp(-rate_ref[:, cols])
        value = (
            key_ref[rows, cols].astype(jnp.float32)
            * part_ref[:, cols].astype(jnp.float32)
            * scale_ref[...]
            * gain_ref[:, cols]
        ).astype(jnp.bfloat16)
        made_ref[:, cols] = value
        wide_ref[side] = value.astype(jnp.float32)
        held = swept(wide_ref.at[side], decay_ref.at[side])
        if not last:
            for m in range(modes):
                held_ref[block, m] = held[m]
            pltpu.make_async_copy(held_ref.at[block], end_ref.at[block], sems.at[1]).start()
            pltpu.make_async_copy(made_ref.at[:, cols], value_ref.at[:, cols], sems.at[2]).start()
        remaining = (sublane_iota() - (SUB - 1)).astype(jnp.float32) * float(STEPS)
        tiles = []
        for group in range(modes // SUB):
            span = range(group * SUB, (group + 1) * SUB)
            state = gathered_sums(
                [held[m] * jnp.exp(row_of(rate_ref, m, cols) * remaining) for m in span]
            )
            if last:
                rate = rate_ref[group * SUB : (group + 1) * SUB, cols]
                state = later_ref[group, block] + jnp.exp(-rate * float(HALF)) * state
            tiles.append(state)
        if last:
            joint = jnp.concatenate(tiles, axis=0).astype(jnp.bfloat16)
            for member in range(GROUP):
                state_ref[member, :, cols] = joint
        else:
            for group, state in enumerate(tiles):
                state_ref[group, block] = state

    lane_blocks(channels, body)
    join.wait()
    if not last:
        pltpu.make_async_copy(held_ref, end_ref, sems.at[1]).wait()
        pltpu.make_async_copy(made_ref, value_ref, sems.at[2]).wait()


def gathered_sums(values):
    row = sublane_iota()
    span = 1
    while span < SUB:
        upper = (row & span) != 0
        values = [
            jnp.where(upper, b, a) + pltpu.roll(jnp.where(upper, a, b), span, axis=0)
            for a, b in zip(values[::2], values[1::2])
        ]
        span *= 2
    return values[0]


def half_states(part, key, near, far, gain, rates, row_start, total_channels, last=()):
    channels = part.shape[1]
    modes = rates.shape[0]
    blocks = channels // LANES
    ends = (blocks, modes, SUB, LANES)
    outputs = [
        shape_of(part.shape, jnp.bfloat16),
        shape_of((GROUP, modes, channels), jnp.bfloat16)
        if last
        else shape_of((modes // SUB, blocks, SUB, LANES), jnp.float32),
        shape_of((2 * HALF, channels), jnp.bfloat16),
    ]
    scratch = [
        pltpu.VMEM((2, HALF, LANES), jnp.float32),
        pltpu.VMEM((HALF, HALF), jnp.float32),
        pltpu.VMEM((2, modes, LANES), jnp.float32),
        pltpu.SemaphoreType.DMA((3,)),
    ]
    if not last:
        outputs += [shape_of(ends, jnp.float32)]
        scratch += [pltpu.VMEM(part.shape, jnp.bfloat16), pltpu.VMEM(ends, jnp.float32)]
    return local_call(
        functools.partial(state_kernel, row_start, total_channels, len(last)),
        "states",
        outputs,
        (part, key, near, far, gain, rates, *last),
        scratch,
        far_in=(7,) if last else (),
        far_out=(2,) if last else (0, 2, 3),
        aliases={7: 2} if last else {},
    )


def member_index():
    return lax.rem(lax.axis_index("ctx"), GROUP)


def group_kernel(span, rate_ref, state_ref, total_ref, before_ref):
    member = member_index()

    def body(block, cols, side):
        decay = jnp.exp(rate_ref[:, cols] * -span)
        held = jnp.zeros_like(decay)
        before = held
        for source in range(GROUP):
            if source > 0:
                before = jnp.where(member == source, held, before)
            held = held * decay + state_ref[source, :, cols].astype(jnp.float32)
        total = held.astype(jnp.bfloat16)
        for level in range(total_ref.shape[0]):
            total_ref[level, :, cols] = total
        before_ref[:, cols] = before

    lane_blocks(rate_ref.shape[1], body)


def group_scan(rates, states, span, levels):
    return local_call(
        functools.partial(group_kernel, float(span)),
        "group",
        [shape_of((levels, *rates.shape), jnp.bfloat16), shape_of(rates.shape, jnp.float32)],
        (rates, states),
    )


def shifted_down(value, count):
    return jnp.where(sublane_iota() >= count, pltpu.roll(value, count, axis=0), 0.0)


def tree_sum(terms):
    while len(terms) > 1:
        odd = terms[len(terms) // 2 * 2 :]
        terms = [a + b for a, b in zip(terms[::2], terms[1::2])] + odd
    return terms[0]


def weights_of(residue_ref, rate_ref):
    rates = rate_ref[...]
    return residue_ref[...] * jnp.sqrt(rates) * jnp.exp(-rates)


def inner_kernel(
    low_ref,
    far_value_ref,
    far_end_ref,
    rate_ref,
    residue_ref,
    skip_ref,
    near_ref,
    out_ref,
    weight_ref,
    wide_ref,
    decay_ref,
    tap_ref,
    made_ref,
    high_ref,
    end_ref,
    sems,
    value_sem,
    near_sem,
):
    modes, channels = rate_ref.shape
    blocks = channels // LANES

    def arriving(block):
        return pltpu.make_async_copy(far_end_ref.at[block], end_ref.at[block], sems.at[block])

    for block in range(blocks):
        arriving(block).start()
    fetch = pltpu.make_async_copy(far_value_ref, high_ref, value_sem)
    fetch.start()
    weight_ref[...] = weights_of(residue_ref, rate_ref)

    def joined(run, spans):
        for span, factor in zip((1, 2, 4), spans):
            run = run + factor * shifted_down(run, span)
        return run

    def prefix_body(block, cols, side):
        decay_ref[side] = jnp.exp(-rate_ref[:, cols])
        wide_ref[side, 0] = low_ref[:, cols].astype(jnp.float32)
        lows = swept(wide_ref.at[side, 0], decay_ref.at[side])
        arriving(block).wait()
        position = sublane_iota().astype(jnp.float32) * float(-STEPS)
        for m in range(modes):
            rate = row_of(rate_ref, m, cols)
            weight = row_of(weight_ref, m, cols)
            spans = [jnp.exp(rate * float(-STEPS * span)) for span in (1, 2, 4)]
            run = joined(lows[m], spans)
            out_ref[block, 0, m] = shifted_down(run, 1) * weight
            carried = jnp.broadcast_to(run[SUB - 1 :], (SUB, LANES))
            run = joined(end_ref[block, m], spans)
            out_ref[block, 1, m] = (
                shifted_down(run, 1) + jnp.exp(rate * position) * carried
            ) * weight

    lane_blocks(channels, prefix_body)
    fetch.wait()

    def short_body(block, cols, side):
        for start in range(0, STEPS, SUB):
            offset = (sublane_iota() + start).astype(jnp.float32)
            terms = []
            for m in range(modes):
                rate = row_of(rate_ref, m, cols)
                factor = row_of(residue_ref, m, cols) * jnp.sqrt(rate)
                terms.append(factor * jnp.exp(-rate * offset))
            tap_ref[side, start : start + SUB, :] = tree_sum(terms)
        for half, value_ref in enumerate((low_ref, high_ref)):
            wide_ref[side, half] = value_ref[:, cols].astype(jnp.float32)
            steps = [wide_ref[side, half, pl.ds(i, SUB, stride=STEPS), :] for i in range(STEPS)]
            skip = jnp.broadcast_to(skip_ref[:, cols], (SUB, LANES))
            sums = [None] * STEPS
            for k in range(STEPS):
                tap = jnp.broadcast_to(tap_ref[side, k : k + 1, :], (SUB, LANES))
                if k == 0:
                    tap = tap + skip
                for i in range(k, STEPS):
                    term = tap * steps[i - k]
                    sums[i] = term if k == 0 else sums[i] + term
            for i in range(STEPS):
                made_ref[block, pl.ds((half * STEPS + i) * SUB, SUB), :] = sums[i]
        pltpu.make_async_copy(made_ref.at[block], near_ref.at[block], near_sem).start()

    lane_blocks(channels, short_body)
    pltpu.make_async_copy(made_ref, near_ref, near_sem).wait()


def inner_part(low, high, high_end, rates, residues, skip):
    modes, channels = rates.shape
    blocks = channels // LANES
    near = shape_of((blocks, 2 * HALF, LANES), jnp.float32)
    return local_call(
        inner_kernel,
        "inner",
        [near, shape_of((blocks, 2, modes, SUB, LANES), jnp.float32)],
        (low, high, high_end, rates, residues, skip),
        [
            pltpu.VMEM(rates.shape, jnp.float32),
            pltpu.VMEM((2, 2, HALF, LANES), jnp.float32),
            pltpu.VMEM((2, modes, LANES), jnp.float32),
            pltpu.VMEM((2, STEPS, LANES), jnp.float32),
            pltpu.VMEM(near.shape, jnp.float32),
            pltpu.VMEM(high.shape, high.dtype),
            pltpu.VMEM(high_end.shape, high_end.dtype),
            pltpu.SemaphoreType.DMA((blocks,)),
            pltpu.SemaphoreType.DMA(()),
            pltpu.SemaphoreType.DMA(()),
        ],
        far_in=(1, 2),
        far_out=(0,),
    )


def output_kernel(
    lag,
    near_ref,
    prefix_ref,
    before_ref,
    totals_ref,
    rate_ref,
    residue_ref,
    query_ref,
    out_ref,
    mixed_ref,
    ready_ref,
    nears_ref,
    queries_ref,
    gain_ref,
    decay_ref,
    weight_ref,
    sems,
    out_sem,
):
    modes = rate_ref.shape[0]
    blocks = near_ref.shape[0]

    def arriving(block):
        return (
            pltpu.make_async_copy(near_ref.at[block], nears_ref.at[block], sems.at[0, block]),
            pltpu.make_async_copy(
                query_ref.at[:, column(block)], queries_ref.at[block], sems.at[1, block]
            ),
        )

    for block in range(blocks):
        for copy in arriving(block):
            copy.start()
    decay_ref[...] = jnp.exp(-rate_ref[...])
    rates = rate_ref[...]
    member = member_index().astype(jnp.float32)
    span = float(2 * HALF)
    level = jnp.exp(rates * (-span * GROUP))
    held = jnp.zeros_like(rates)
    earlier = held
    row = lax.div(lax.axis_index("ctx"), GROUP)
    for source in range(totals_ref.shape[0] - 1):
        held = held * level + totals_ref[source].astype(jnp.float32)
        earlier = jnp.where(row == source + 1, held, earlier)
    start = before_ref[...] + jnp.exp(rates * (-span * member)) * earlier
    weight_ref[...] = weights_of(residue_ref, rate_ref) * start

    def corrected(block, side):
        cols = column(block)
        every = pl.ds(0, LANES)
        for group in range(modes // SUB):
            span = slice(group * SUB, (group + 1) * SUB)
            gain = weight_ref[span, cols]
            gain_ref[side, 0, span, :] = gain
            gain_ref[side, 1, span, :] = gain * jnp.exp(rate_ref[span, cols] * float(-HALF))
        position = sublane_iota().astype(jnp.float32) * float(-STEPS)
        decay = [row_of(decay_ref, m, cols) for m in range(modes)]
        held = [[], []]
        for m in range(modes):
            reach = jnp.exp(row_of(rate_ref, m, cols) * position)
            for half in range(2):
                gain = row_of(gain_ref.at[side, half], m, every)
                held[half].append(prefix_ref[block, half, m] + reach * gain)
        for i in range(STEPS):
            for half in range(2):
                if i > 0:
                    held[half] = [h * d for h, d in zip(held[half], decay)]
                mixed_ref[block, pl.ds((half * STEPS + i) * SUB, SUB), :] = tree_sum(held[half])

    def finished(block):
        cols = column(block)
        for copy in arriving(block):
            copy.wait()
        nears_ref[block] = nears_ref[block] + mixed_ref[block]
        for half in range(2):
            for s in range(SUB):
                rows = pl.ds(half * HALF + s * STEPS, STEPS)
                mixed = nears_ref[block, pl.ds(half * HALF + s, STEPS, stride=SUB), :]
                ready_ref[rows, cols] = (
                    queries_ref[block, rows, :].astype(jnp.float32) * mixed
                ).astype(jnp.bfloat16)
        pltpu.make_async_copy(ready_ref.at[:, cols], out_ref.at[:, cols], out_sem).start()

    for block in range(lag):
        corrected(block, block % 2)

    def step(pair, carry):
        for side in range(2):
            block = lag + pair * 2 + side
            finished(block - lag)
            corrected(block, side)
        return carry

    lax.fori_loop(0, (blocks - lag) // 2, step, 0)
    for block in range(blocks - lag, blocks):
        finished(block)
    pltpu.make_async_copy(ready_ref, out_ref, out_sem).wait()


def long_output(near, prefix, before, earlier, rates, residues, query):
    blocks = near.shape[0]
    return local_call(
        functools.partial(output_kernel, 2),
        "output",
        shape_of(query.shape, jnp.bfloat16),
        (near, prefix, before, earlier, rates, residues, query),
        [
            pltpu.VMEM(near.shape, jnp.float32),
            pltpu.VMEM(query.shape, jnp.bfloat16),
            pltpu.VMEM(near.shape, jnp.float32),
            pltpu.VMEM((blocks, 2 * HALF, LANES), jnp.bfloat16),
            pltpu.VMEM((2, 2, *rates.shape[:1], LANES), jnp.float32),
            pltpu.VMEM(rates.shape, jnp.float32),
            pltpu.VMEM(rates.shape, jnp.float32),
            pltpu.SemaphoreType.DMA((2, blocks)),
            pltpu.SemaphoreType.DMA(()),
        ],
        far_in=(0, 6),
        far_out=(0,),
    )


def summed_with_pair(value):
    return value + lax.ppermute(value, "tp", [(0, 1), (1, 0), (2, 3), (3, 2)])


def across_pairs(value):
    return lax.ppermute(value, "tp", [(0, 2), (2, 0), (1, 3), (3, 1)])


def on_device(
    query_one,
    key_one,
    value_one,
    residual_in,
    medium_taps,
    skip_one,
    norm_gain,
    query_two,
    key_two,
    residues,
    decay_rates,
    skip_two,
):
    rows, channels = query_one.shape
    forward, backward = transform_tables(2 * HALF)
    tables = (
        jnp.asarray(np.concatenate(split_table(forward), axis=0)),
        jnp.asarray(np.concatenate(split_table(backward), axis=0)),
    )
    skip_row = skip_one[None, :]
    gain_row = norm_gain[None, :]
    skip_long = skip_two[None, :]
    product_high = key_one[HALF:] * value_one[HALF:]
    count = lax.axis_size("ctx")
    before = lax.ppermute(product_high, "ctx", [(d, d + 1) for d in range(count - 1)])
    high, square_high, product_low, *spectrum = upper_block(
        product_high, key_one, value_one, medium_taps, tables, query_one, residual_in, skip_row
    )
    near_high = summed_with_pair(square_high)
    far_high = across_pairs(near_high)
    total_channels = channels * lax.axis_size("tp")
    value_high, state_high, residual_out, end_high = half_states(
        high, key_two, near_high, far_high, gain_row, decay_rates, HALF, total_channels
    )
    before, state_high = lax.optimization_barrier((before, state_high))
    low, square_low = lower_block(
        before, product_low, spectrum, query_one, residual_in, skip_row, tables
    )
    near_low = summed_with_pair(square_low)
    far_low = across_pairs(near_low)
    value_low, state, residual_out = half_states(
        low,
        key_two,
        near_low,
        far_low,
        gain_row,
        decay_rates,
        0,
        total_channels,
        (state_high, residual_out),
    )
    members = [
        [first + k for k in range(GROUP)] for first in range(0, lax.axis_size("ctx"), GROUP)
    ]
    gathered = lax.all_to_all(
        state, "ctx", split_axis=0, concat_axis=0, tiled=True, axis_index_groups=members
    )
    near, prefix = inner_part(
        value_low, value_high, end_high, decay_rates, residues, skip_long
    )
    gathered, near, prefix = lax.optimization_barrier((gathered, near, prefix))
    total, before_here = group_scan(decay_rates, gathered, rows, count // GROUP)
    columns = [list(range(first, count, GROUP)) for first in range(GROUP)]
    earlier = lax.all_to_all(
        total, "ctx", split_axis=0, concat_axis=0, tiled=True, axis_index_groups=columns
    )
    result = long_output(
        near, prefix, before_here, earlier, decay_rates, residues, query_two
    )
    return (residual_out, result)


def solution(mesh):
    in_specs = (
        P("ctx", "tp"),
        P("ctx", "tp"),
        P("ctx", "tp"),
        P("ctx", "tp"),
        P(None, "tp"),
        P("tp"),
        P("tp"),
        P("ctx", "tp"),
        P("ctx", "tp"),
        P(None, "tp"),
        P(None, "tp"),
        P("tp"),
    )
    out_specs = (P("ctx", "tp"), P("ctx", "tp"))
    return jax.shard_map(
        on_device, mesh=mesh, in_specs=in_specs, out_specs=out_specs, check_vma=False
    )
```

```python
import functools
import math

import jax
import jax.numpy as jnp
import numpy as np
from jax import lax
from jax.experimental import pallas as pl
from jax.experimental.pallas import tpu as pltpu
from jax.sharding import PartitionSpec as P

HALF = 128
LANES = 128
SUB = 8
STEPS = HALF // SUB
WIDE = 256
GROUP = 8


def split_table(table):
    upper = table.astype(jnp.bfloat16)
    lower = (table - upper.astype(np.float64)).astype(jnp.bfloat16)
    return upper, lower


def transform_tables(count):
    half = count // 2
    freq = np.arange(half)[:, None]
    time = np.arange(count)[None, :]
    angle = 2.0 * math.pi * ((freq * time) % count) / count
    even = np.cos(angle)
    odd = -np.sin(angle)
    odd[0] = np.where(np.arange(count) % 2 == 0, 1.0, -1.0)
    forward = np.concatenate([even, odd], axis=0)
    weight = np.full((half, 1), 2.0 / count)
    weight[0] = 1.0 / count
    backward = np.concatenate([even * weight, odd * weight], axis=0).T[half:]
    return forward, backward


def dot32(left, right):
    return jnp.dot(left, right, preferred_element_type=jnp.float32)


HBM = pltpu.HBM


def local_call(
    kernel, name, out_shape, operands, scratch=(), far_in=(), far_out=(), aliases={}
):
    outputs = out_shape if isinstance(out_shape, list) else [out_shape]
    near = pl.BlockSpec(memory_space=pltpu.VMEM)
    far = pl.BlockSpec(memory_space=HBM)
    call = pl.pallas_call(
        kernel,
        in_specs=[far if k in far_in else near for k in range(len(operands))],
        out_specs=[far if k in far_out else near for k in range(len(outputs))],
        out_shape=[
            (HBM if k in far_out else pltpu.VMEM)(o.shape, o.dtype) for k, o in enumerate(outputs)
        ],
        scratch_shapes=list(scratch),
        compiler_params=pltpu.CompilerParams(vmem_limit_bytes=8 << 20),
        input_output_aliases=aliases,
        name=name,
    )
    results = call(
        *[
            pltpu.with_memory_space_constraint(operand, HBM if k in far_in else pltpu.VMEM)
            for k, operand in enumerate(operands)
        ]
    )
    return results if isinstance(out_shape, list) else results[0]


def shape_of(shape, dtype):
    return jax.ShapeDtypeStruct(shape, dtype)


def forward_part(fwd, signal):
    count = 2 * HALF
    both = dot32(fwd, signal)
    return both[:count] + both[count:]


def joint_parts(spec, taps):
    even, cross, last = taps
    sig_even, sig_odd = spec[:HALF], spec[HALF:]
    joint = jnp.concatenate(
        [sig_even * even - sig_odd * cross, sig_even * cross + sig_odd * last], axis=0
    )
    joint_hi = joint.astype(jnp.bfloat16)
    return joint_hi, (joint - joint_hi.astype(jnp.float32)).astype(jnp.bfloat16)


def backward_part(bwd, joint_hi, joint_lo):
    back = dot32(bwd, joint_hi)
    return back[:HALF] + back[HALF:] + dot32(bwd[:HALF], joint_lo)


def gated(filtered, here, skip, query, resid):
    mixed = filtered + skip * here.astype(jnp.float32)
    return (resid.astype(jnp.float32) + query.astype(jnp.float32) * mixed).astype(jnp.bfloat16)


def filtered_result(spec, taps, here, skip, query, resid, bwd):
    return gated(backward_part(bwd, *joint_parts(spec, taps)), here, skip, query, resid)


def squares_added(total, result):
    wide = result.astype(jnp.float32)
    squares = wide * wide
    for lane in range(0, WIDE, LANES):
        part = squares[:, lane : lane + LANES]
        total = part if total is None else total + part
    return total


def write_squares(total, square_ref):
    summed = jnp.sum(total.T, axis=0, keepdims=True)
    square_ref[...] = jnp.broadcast_to(summed, square_ref.shape)


def upper_kernel(
    here_ref,
    key_far,
    value_far,
    taps_far,
    fwd_far,
    bwd_far,
    query_far,
    resid_far,
    skip_far,
    out_ref,
    square_ref,
    before_ref,
    even_ref,
    cross_ref,
    last_ref,
    key_ref,
    value_ref,
    taps_ref,
    fwd_ref,
    bwd_ref,
    query_ref,
    resid_ref,
    skip_ref,
    sems,
):
    rows = pl.ds(HALF, HALF)
    first_rows = pl.ds(0, HALF)
    copies = [
        pltpu.make_async_copy(source, target, sems.at[k])
        for k, (source, target) in enumerate(
            (
                (fwd_far, fwd_ref),
                (taps_far, taps_ref),
                (key_far.at[first_rows, :], key_ref),
                (value_far.at[first_rows, :], value_ref),
                (bwd_far, bwd_ref),
                (query_far.at[rows, :], query_ref),
                (resid_far.at[rows, :], resid_ref),
                (skip_far, skip_ref),
            )
        )
    ]
    for copy in copies:
        copy.start()
    total = None
    starts = list(range(0, here_ref.shape[1], WIDE))
    specs = {}
    for index in range(len(starts) + 2):
        if index < len(starts):
            cols = pl.ds(starts[index], WIDE)
            if index == 0:
                copies[0].wait()
                copies[1].wait()
            spec = forward_part(fwd_ref[:, :HALF], taps_ref[:, cols])
            even, odd = spec[:HALF], spec[HALF:]
            first = lax.broadcasted_iota(jnp.int32, even.shape, 0) == 0
            even_ref[:, cols] = even
            cross_ref[:, cols] = jnp.where(first, 0.0, odd)
            last_ref[:, cols] = jnp.where(first, odd, even)
        if 1 <= index <= len(starts):
            cols = pl.ds(starts[index - 1], WIDE)
            if index == 1:
                copies[2].wait()
                copies[3].wait()
            before = (
                key_ref[:, cols].astype(jnp.float32) * value_ref[:, cols].astype(jnp.float32)
            ).astype(jnp.bfloat16)
            before_ref[:, cols] = before
            signal = jnp.concatenate([before, here_ref[:, cols]], axis=0)
            specs[index - 1] = forward_part(fwd_ref[...], signal)
        if index >= 2:
            cols = pl.ds(starts[index - 2], WIDE)
            if index == 2:
                for copy in copies[4:]:
                    copy.wait()
            result = filtered_result(
                specs.pop(index - 2),
                (even_ref[:, cols], cross_ref[:, cols], last_ref[:, cols]),
                here_ref[:, cols],
                skip_ref[:, cols],
                query_ref[:, cols],
                resid_ref[:, cols],
                bwd_ref[...],
            )
            out_ref[:, cols] = result
            total = squares_added(total, result)
    write_squares(total, square_ref)


def upper_block(here, key, value, taps, tables, query, resid, skip):
    half = shape_of(here.shape, jnp.bfloat16)
    spectrum = shape_of(taps.shape, jnp.float32)
    return local_call(
        upper_kernel,
        "upper",
        [half, shape_of((SUB, HALF), jnp.float32), half, spectrum, spectrum, spectrum],
        (here, key, value, taps, *tables, query, resid, skip),
        [
            pltpu.VMEM(here.shape, jnp.bfloat16),
            pltpu.VMEM(here.shape, jnp.bfloat16),
            pltpu.VMEM(taps.shape, jnp.bfloat16),
            pltpu.VMEM(tables[0].shape, jnp.bfloat16),
            pltpu.VMEM(tables[1].shape, jnp.bfloat16),
            pltpu.VMEM(here.shape, jnp.bfloat16),
            pltpu.VMEM(here.shape, jnp.bfloat16),
            pltpu.VMEM(skip.shape, jnp.float32),
            pltpu.SemaphoreType.DMA((8,)),
        ],
        far_in=tuple(range(1, 9)),
    )


def lower_kernel(
    before_ref,
    here_ref,
    even_ref,
    cross_ref,
    last_ref,
    query_ref,
    resid_ref,
    skip_ref,
    fwd_ref,
    bwd_ref,
    out_ref,
    square_ref,
):
    rows = pl.ds(0, HALF)
    total = None
    starts = list(range(0, here_ref.shape[1], WIDE))
    specs, joints, backs = {}, {}, {}
    for index in range(len(starts) + 3):
        chunk = index - 3
        if chunk >= 0:
            cols = pl.ds(starts[chunk], WIDE)
            result = gated(
                backs.pop(chunk),
                here_ref[:, cols],
                skip_ref[:, cols],
                query_ref[rows, cols],
                resid_ref[rows, cols],
            )
            out_ref[:, cols] = result
            total = squares_added(total, result)
        chunk = index - 2
        if 0 <= chunk < len(starts):
            backs[chunk] = backward_part(bwd_ref[...], *joints.pop(chunk))
        chunk = index
        if chunk < len(starts):
            cols = pl.ds(starts[chunk], WIDE)
            signal = jnp.concatenate([before_ref[:, cols], here_ref[:, cols]], axis=0)
            specs[chunk] = forward_part(fwd_ref[...], signal)
        chunk = index - 1
        if 0 <= chunk < len(starts):
            cols = pl.ds(starts[chunk], WIDE)
            taps = (even_ref[:, cols], cross_ref[:, cols], last_ref[:, cols])
            joints[chunk] = joint_parts(specs.pop(chunk), taps)
    write_squares(total, square_ref)


def lower_block(before, here, spectrum, query, resid, skip, tables):
    return local_call(
        lower_kernel,
        "lower",
        [shape_of(here.shape, jnp.bfloat16), shape_of((SUB, HALF), jnp.float32)],
        (before, here, *spectrum, query, resid, skip, *tables),
    )


def sublane_iota():
    return lax.broadcasted_iota(jnp.int32, (SUB, LANES), 0)


def row_of(ref, row, cols):
    return jnp.broadcast_to(ref[row : row + 1, cols], (SUB, LANES))


def lane_blocks(channels, body):
    def step(pair, carry):
        for side in range(2):
            block = pair * 2 + side
            body(block, column(block), side)
        return carry

    lax.fori_loop(0, channels // (2 * LANES), step, 0)


def column(block):
    return pl.ds(pl.multiple_of(block * LANES, LANES), LANES)


def swept(wide_ref, decay_ref):
    decay = [row_of(decay_ref, m, pl.ds(0, LANES)) for m in range(decay_ref.shape[0])]
    held = None
    for i in range(STEPS):
        step = wide_ref[pl.ds(i, SUB, stride=STEPS), :]
        held = [step] * len(decay) if i == 0 else [h * d + step for h, d in zip(held, decay)]
    return held


def ready_kernel(part_ref, key_ref, gain_ref, rate_ref, scaled_ref, reach_ref):
    remaining = (sublane_iota() - (SUB - 1)).astype(jnp.float32) * float(STEPS)

    def body(block, cols, side):
        scaled_ref[:, cols] = (
            key_ref[:HALF, cols].astype(jnp.float32)
            * part_ref[:, cols].astype(jnp.float32)
            * gain_ref[:, cols]
        )
        for m in range(rate_ref.shape[0]):
            reach_ref[block, m] = jnp.exp(row_of(rate_ref, m, cols) * remaining)

    lane_blocks(rate_ref.shape[1], body)


def made_ready(part, key, gain, rates):
    modes, channels = rates.shape
    return local_call(
        ready_kernel,
        "ready",
        [
            shape_of(part.shape, jnp.float32),
            shape_of((channels // LANES, modes, SUB, LANES), jnp.float32),
        ],
        (part, key, gain, rates),
    )


def state_kernel(row_start, total_channels, last, *refs):
    if last:
        part_ref, near_ref, far_ref, rate_ref, scaled_ref, reach_ref, later_ref = refs[:7]
        value_ref, state_ref, joined_ref, wide_ref, scale_ref, decay_ref, sems = refs[8:]
        made_ref = value_ref
    else:
        part_ref, near_ref, far_ref, rate_ref, key_ref, gain_ref = refs[:6]
        value_ref, state_ref, joined_ref, end_ref = refs[6:10]
        wide_ref, scale_ref, decay_ref, sems, made_ref, held_ref = refs[10:]
    join = pltpu.make_async_copy(
        part_ref, joined_ref.at[pl.ds(row_start, HALF), :], sems.at[0]
    )
    join.start()
    modes, channels = rate_ref.shape
    rows = pl.ds(row_start, HALF)
    scale = lax.rsqrt((near_ref[...] + far_ref[...]) / total_channels + 1e-05)
    scale_ref[...] = jnp.broadcast_to(scale[:1], (HALF, HALF)).T

    def body(block, cols, side):
        decay_ref[side] = jnp.exp(-rate_ref[:, cols])
        if last:
            scaled = scaled_ref[:, cols]
        else:
            scaled = (
                key_ref[rows, cols].astype(jnp.float32)
                * part_ref[:, cols].astype(jnp.float32)
                * gain_ref[:, cols]
            )
        value = (scaled * scale_ref[...]).astype(jnp.bfloat16)
        made_ref[:, cols] = value
        wide_ref[side] = value.astype(jnp.float32)
        held = swept(wide_ref.at[side], decay_ref.at[side])
        if not last:
            for m in range(modes):
                held_ref[block, m] = held[m]
            pltpu.make_async_copy(held_ref.at[block], end_ref.at[block], sems.at[1]).start()
            pltpu.make_async_copy(made_ref.at[:, cols], value_ref.at[:, cols], sems.at[2]).start()
        remaining = (sublane_iota() - (SUB - 1)).astype(jnp.float32) * float(STEPS)
        tiles = []
        for group in range(modes // SUB):
            span = range(group * SUB, (group + 1) * SUB)
            if last:
                reach = [reach_ref[block, m] for m in span]
            else:
                reach = [jnp.exp(row_of(rate_ref, m, cols) * remaining) for m in span]
            state = gathered_sums([held[m] * r for m, r in zip(span, reach)])
            if last:
                rate = rate_ref[group * SUB : (group + 1) * SUB, cols]
                state = later_ref[group, block] + jnp.exp(-rate * float(HALF)) * state
            tiles.append(state)
        if last:
            joint = jnp.concatenate(tiles, axis=0).astype(jnp.bfloat16)
            for member in range(GROUP):
                state_ref[member, :, cols] = joint
        else:
            for group, state in enumerate(tiles):
                state_ref[group, block] = state

    lane_blocks(channels, body)
    join.wait()
    if not last:
        pltpu.make_async_copy(held_ref, end_ref, sems.at[1]).wait()
        pltpu.make_async_copy(made_ref, value_ref, sems.at[2]).wait()


def gathered_sums(values):
    row = sublane_iota()
    span = 1
    while span < SUB:
        upper = (row & span) != 0
        values = [
            jnp.where(upper, b, a) + pltpu.roll(jnp.where(upper, a, b), span, axis=0)
            for a, b in zip(values[::2], values[1::2])
        ]
        span *= 2
    return values[0]


def half_states(part, near, far, rates, extra, row_start, total_channels, last=()):
    channels = part.shape[1]
    modes = rates.shape[0]
    blocks = channels // LANES
    ends = (blocks, modes, SUB, LANES)
    outputs = [
        shape_of(part.shape, jnp.bfloat16),
        shape_of((GROUP, modes, channels), jnp.bfloat16)
        if last
        else shape_of((modes // SUB, blocks, SUB, LANES), jnp.float32),
        shape_of((2 * HALF, channels), jnp.bfloat16),
    ]
    scratch = [
        pltpu.VMEM((2, HALF, LANES), jnp.float32),
        pltpu.VMEM((HALF, HALF), jnp.float32),
        pltpu.VMEM((2, modes, LANES), jnp.float32),
        pltpu.SemaphoreType.DMA((3,)),
    ]
    if not last:
        outputs += [shape_of(ends, jnp.float32)]
        scratch += [pltpu.VMEM(part.shape, jnp.bfloat16), pltpu.VMEM(ends, jnp.float32)]
    return local_call(
        functools.partial(state_kernel, row_start, total_channels, len(last)),
        "states",
        outputs,
        (part, near, far, rates, *extra, *last),
        scratch,
        far_in=(7,) if last else (),
        far_out=(2,) if last else (0, 2, 3),
        aliases={7: 2} if last else {},
    )


def member_index():
    return lax.rem(lax.axis_index("ctx"), GROUP)


def group_kernel(span, rate_ref, state_ref, total_ref, before_ref):
    member = member_index()

    def body(block, cols, side):
        decay = jnp.exp(rate_ref[:, cols] * -span)
        held = jnp.zeros_like(decay)
        before = held
        for source in range(GROUP):
            if source > 0:
                before = jnp.where(member == source, held, before)
            held = held * decay + state_ref[source, :, cols].astype(jnp.float32)
        total = held.astype(jnp.bfloat16)
        for level in range(total_ref.shape[0]):
            total_ref[level, :, cols] = total
        before_ref[:, cols] = before

    lane_blocks(rate_ref.shape[1], body)


def group_scan(rates, states, span, levels):
    return local_call(
        functools.partial(group_kernel, float(span)),
        "group",
        [shape_of((levels, *rates.shape), jnp.bfloat16), shape_of(rates.shape, jnp.float32)],
        (rates, states),
    )


def shifted_down(value, count):
    return jnp.where(sublane_iota() >= count, pltpu.roll(value, count, axis=0), 0.0)


def tree_sum(terms):
    while len(terms) > 1:
        odd = terms[len(terms) // 2 * 2 :]
        terms = [a + b for a, b in zip(terms[::2], terms[1::2])] + odd
    return terms[0]


def weights_of(residue_ref, rate_ref):
    rates = rate_ref[...]
    return residue_ref[...] * jnp.sqrt(rates) * jnp.exp(-rates)


def inner_kernel(
    low_ref,
    far_value_ref,
    far_end_ref,
    rate_ref,
    residue_ref,
    skip_ref,
    near_ref,
    out_ref,
    weight_ref,
    wide_ref,
    decay_ref,
    tap_ref,
    made_ref,
    high_ref,
    end_ref,
    sems,
    value_sem,
    near_sem,
):
    modes, channels = rate_ref.shape
    blocks = channels // LANES

    def arriving(block):
        return pltpu.make_async_copy(far_end_ref.at[block], end_ref.at[block], sems.at[block])

    for block in range(blocks):
        arriving(block).start()
    fetch = pltpu.make_async_copy(far_value_ref, high_ref, value_sem)
    fetch.start()
    weight_ref[...] = weights_of(residue_ref, rate_ref)

    def joined(run, spans):
        for span, factor in zip((1, 2, 4), spans):
            run = run + factor * shifted_down(run, span)
        return run

    def prefix_body(block, cols, side):
        decay_ref[side] = jnp.exp(-rate_ref[:, cols])
        wide_ref[side, 0] = low_ref[:, cols].astype(jnp.float32)
        lows = swept(wide_ref.at[side, 0], decay_ref.at[side])
        arriving(block).wait()
        position = sublane_iota().astype(jnp.float32) * float(-STEPS)
        for m in range(modes):
            rate = row_of(rate_ref, m, cols)
            weight = row_of(weight_ref, m, cols)
            spans = [jnp.exp(rate * float(-STEPS * span)) for span in (1, 2, 4)]
            run = joined(lows[m], spans)
            out_ref[block, 0, m] = shifted_down(run, 1) * weight
            carried = jnp.broadcast_to(run[SUB - 1 :], (SUB, LANES))
            run = joined(end_ref[block, m], spans)
            out_ref[block, 1, m] = (
                shifted_down(run, 1) + jnp.exp(rate * position) * carried
            ) * weight

    lane_blocks(channels, prefix_body)
    fetch.wait()

    def short_body(block, cols, side):
        for start in range(0, STEPS, SUB):
            offset = (sublane_iota() + start).astype(jnp.float32)
            terms = []
            for m in range(modes):
                rate = row_of(rate_ref, m, cols)
                factor = row_of(residue_ref, m, cols) * jnp.sqrt(rate)
                terms.append(factor * jnp.exp(-rate * offset))
            tap_ref[side, start : start + SUB, :] = tree_sum(terms)
        for half, value_ref in enumerate((low_ref, high_ref)):
            wide_ref[side, half] = value_ref[:, cols].astype(jnp.float32)
            steps = [wide_ref[side, half, pl.ds(i, SUB, stride=STEPS), :] for i in range(STEPS)]
            skip = jnp.broadcast_to(skip_ref[:, cols], (SUB, LANES))
            sums = [None] * STEPS
            for k in range(STEPS):
                tap = jnp.broadcast_to(tap_ref[side, k : k + 1, :], (SUB, LANES))
                if k == 0:
                    tap = tap + skip
                for i in range(k, STEPS):
                    term = tap * steps[i - k]
                    sums[i] = term if k == 0 else sums[i] + term
            for i in range(STEPS):
                made_ref[block, pl.ds((half * STEPS + i) * SUB, SUB), :] = sums[i]
        pltpu.make_async_copy(made_ref.at[block], near_ref.at[block], near_sem).start()

    lane_blocks(channels, short_body)
    pltpu.make_async_copy(made_ref, near_ref, near_sem).wait()


def inner_part(low, high, high_end, rates, residues, skip):
    modes, channels = rates.shape
    blocks = channels // LANES
    near = shape_of((blocks, 2 * HALF, LANES), jnp.float32)
    return local_call(
        inner_kernel,
        "inner",
        [near, shape_of((blocks, 2, modes, SUB, LANES), jnp.float32)],
        (low, high, high_end, rates, residues, skip),
        [
            pltpu.VMEM(rates.shape, jnp.float32),
            pltpu.VMEM((2, 2, HALF, LANES), jnp.float32),
            pltpu.VMEM((2, modes, LANES), jnp.float32),
            pltpu.VMEM((2, STEPS, LANES), jnp.float32),
            pltpu.VMEM(near.shape, jnp.float32),
            pltpu.VMEM(high.shape, high.dtype),
            pltpu.VMEM(high_end.shape, high_end.dtype),
            pltpu.SemaphoreType.DMA((blocks,)),
            pltpu.SemaphoreType.DMA(()),
            pltpu.SemaphoreType.DMA(()),
        ],
        far_in=(1, 2),
        far_out=(0,),
    )


def output_kernel(
    lag,
    near_ref,
    prefix_ref,
    before_ref,
    totals_ref,
    rate_ref,
    residue_ref,
    query_ref,
    out_ref,
    mixed_ref,
    ready_ref,
    nears_ref,
    queries_ref,
    gain_ref,
    decay_ref,
    weight_ref,
    sems,
    out_sem,
):
    modes = rate_ref.shape[0]
    blocks = near_ref.shape[0]

    def arriving(block):
        return (
            pltpu.make_async_copy(near_ref.at[block], nears_ref.at[block], sems.at[0, block]),
            pltpu.make_async_copy(
                query_ref.at[:, column(block)], queries_ref.at[block], sems.at[1, block]
            ),
        )

    for block in range(blocks):
        for copy in arriving(block):
            copy.start()
    decay_ref[...] = jnp.exp(-rate_ref[...])
    rates = rate_ref[...]
    member = member_index().astype(jnp.float32)
    span = float(2 * HALF)
    level = jnp.exp(rates * (-span * GROUP))
    held = jnp.zeros_like(rates)
    earlier = held
    row = lax.div(lax.axis_index("ctx"), GROUP)
    for source in range(totals_ref.shape[0] - 1):
        held = held * level + totals_ref[source].astype(jnp.float32)
        earlier = jnp.where(row == source + 1, held, earlier)
    start = before_ref[...] + jnp.exp(rates * (-span * member)) * earlier
    weight_ref[...] = weights_of(residue_ref, rate_ref) * start

    def corrected(block, side):
        cols = column(block)
        every = pl.ds(0, LANES)
        for group in range(modes // SUB):
            span = slice(group * SUB, (group + 1) * SUB)
            gain = weight_ref[span, cols]
            gain_ref[side, 0, span, :] = gain
            gain_ref[side, 1, span, :] = gain * jnp.exp(rate_ref[span, cols] * float(-HALF))
        position = sublane_iota().astype(jnp.float32) * float(-STEPS)
        decay = [row_of(decay_ref, m, cols) for m in range(modes)]
        held = [[], []]
        for m in range(modes):
            reach = jnp.exp(row_of(rate_ref, m, cols) * position)
            for half in range(2):
                gain = row_of(gain_ref.at[side, half], m, every)
                held[half].append(prefix_ref[block, half, m] + reach * gain)
        for i in range(STEPS):
            for half in range(2):
                if i > 0:
                    held[half] = [h * d for h, d in zip(held[half], decay)]
                mixed_ref[block, pl.ds((half * STEPS + i) * SUB, SUB), :] = tree_sum(held[half])

    def finished(block):
        cols = column(block)
        for copy in arriving(block):
            copy.wait()
        nears_ref[block] = nears_ref[block] + mixed_ref[block]
        for half in range(2):
            for s in range(SUB):
                rows = pl.ds(half * HALF + s * STEPS, STEPS)
                mixed = nears_ref[block, pl.ds(half * HALF + s, STEPS, stride=SUB), :]
                ready_ref[rows, cols] = (
                    queries_ref[block, rows, :].astype(jnp.float32) * mixed
                ).astype(jnp.bfloat16)
        pltpu.make_async_copy(ready_ref.at[:, cols], out_ref.at[:, cols], out_sem).start()

    for block in range(lag):
        corrected(block, block % 2)

    def step(pair, carry):
        for side in range(2):
            block = lag + pair * 2 + side
            finished(block - lag)
            corrected(block, side)
        return carry

    lax.fori_loop(0, (blocks - lag) // 2, step, 0)
    for block in range(blocks - lag, blocks):
        finished(block)
    pltpu.make_async_copy(ready_ref, out_ref, out_sem).wait()


def long_output(near, prefix, before, earlier, rates, residues, query):
    blocks = near.shape[0]
    return local_call(
        functools.partial(output_kernel, 2),
        "output",
        shape_of(query.shape, jnp.bfloat16),
        (near, prefix, before, earlier, rates, residues, query),
        [
            pltpu.VMEM(near.shape, jnp.float32),
            pltpu.VMEM(query.shape, jnp.bfloat16),
            pltpu.VMEM(near.shape, jnp.float32),
            pltpu.VMEM((blocks, 2 * HALF, LANES), jnp.bfloat16),
            pltpu.VMEM((2, 2, *rates.shape[:1], LANES), jnp.float32),
            pltpu.VMEM(rates.shape, jnp.float32),
            pltpu.VMEM(rates.shape, jnp.float32),
            pltpu.SemaphoreType.DMA((2, blocks)),
            pltpu.SemaphoreType.DMA(()),
        ],
        far_in=(0, 6),
        far_out=(0,),
    )


def summed_with_pair(value):
    return value + lax.ppermute(value, "tp", [(0, 1), (1, 0), (2, 3), (3, 2)])


def across_pairs(value):
    return lax.ppermute(value, "tp", [(0, 2), (2, 0), (1, 3), (3, 1)])


def on_device(
    query_one,
    key_one,
    value_one,
    residual_in,
    medium_taps,
    skip_one,
    norm_gain,
    query_two,
    key_two,
    residues,
    decay_rates,
    skip_two,
):
    rows, channels = query_one.shape
    forward, backward = transform_tables(2 * HALF)
    tables = (
        jnp.asarray(np.concatenate(split_table(forward), axis=0)),
        jnp.asarray(np.concatenate(split_table(backward), axis=0)),
    )
    skip_row = skip_one[None, :]
    gain_row = norm_gain[None, :]
    skip_long = skip_two[None, :]
    product_high = key_one[HALF:] * value_one[HALF:]
    count = lax.axis_size("ctx")
    before = lax.ppermute(product_high, "ctx", [(d, d + 1) for d in range(count - 1)])
    high, square_high, product_low, *spectrum = upper_block(
        product_high, key_one, value_one, medium_taps, tables, query_one, residual_in, skip_row
    )
    near_high = summed_with_pair(square_high)
    far_high = across_pairs(near_high)
    total_channels = channels * lax.axis_size("tp")
    value_high, state_high, residual_out, end_high = half_states(
        high, near_high, far_high, decay_rates, (key_two, gain_row), HALF, total_channels
    )
    before, state_high = lax.optimization_barrier((before, state_high))
    low, square_low = lower_block(
        before, product_low, spectrum, query_one, residual_in, skip_row, tables
    )
    near_low = summed_with_pair(square_low)
    near_low, low = lax.optimization_barrier((near_low, low))
    far_low = across_pairs(near_low)
    ready = made_ready(low, key_two, gain_row, decay_rates)
    value_low, state, residual_out = half_states(
        low,
        near_low,
        far_low,
        decay_rates,
        ready,
        0,
        total_channels,
        (state_high, residual_out),
    )
    members = [
        [first + k for k in range(GROUP)] for first in range(0, lax.axis_size("ctx"), GROUP)
    ]
    gathered = lax.all_to_all(
        state, "ctx", split_axis=0, concat_axis=0, tiled=True, axis_index_groups=members
    )
    near, prefix = inner_part(
        value_low, value_high, end_high, decay_rates, residues, skip_long
    )
    gathered, near, prefix = lax.optimization_barrier((gathered, near, prefix))
    total, before_here = group_scan(decay_rates, gathered, rows, count // GROUP)
    columns = [list(range(first, count, GROUP)) for first in range(GROUP)]
    earlier = lax.all_to_all(
        total, "ctx", split_axis=0, concat_axis=0, tiled=True, axis_index_groups=columns
    )
    result = long_output(
        near, prefix, before_here, earlier, decay_rates, residues, query_two
    )
    return (residual_out, result)


def solution(mesh):
    in_specs = (
        P("ctx", "tp"),
        P("ctx", "tp"),
        P("ctx", "tp"),
        P("ctx", "tp"),
        P(None, "tp"),
        P("tp"),
        P("tp"),
        P("ctx", "tp"),
        P("ctx", "tp"),
        P(None, "tp"),
        P(None, "tp"),
        P("tp"),
    )
    out_specs = (P("ctx", "tp"), P("ctx", "tp"))
    return jax.shard_map(
        on_device, mesh=mesh, in_specs=in_specs, out_specs=out_specs, check_vma=False
    )
```

```python
import functools
import math

import jax
import jax.numpy as jnp
import numpy as np
from jax import lax
from jax.experimental import pallas as pl
from jax.experimental.pallas import tpu as pltpu
from jax.sharding import PartitionSpec as P

HALF = 128
LANES = 128
SUB = 8
STEPS = HALF // SUB
WIDE = 512
GROUP = 8


def split_table(table):
    upper = table.astype(jnp.bfloat16)
    lower = (table - upper.astype(np.float64)).astype(jnp.bfloat16)
    return upper, lower


def transform_tables(count):
    half = count // 2
    freq = np.arange(half)[:, None]
    time = np.arange(count)[None, :]
    angle = 2.0 * math.pi * ((freq * time) % count) / count
    even = np.cos(angle)
    odd = -np.sin(angle)
    odd[0] = np.where(np.arange(count) % 2 == 0, 1.0, -1.0)
    forward = np.concatenate([even, odd], axis=0)
    weight = np.full((half, 1), 2.0 / count)
    weight[0] = 1.0 / count
    backward = np.concatenate([even * weight, odd * weight], axis=0).T[half:]
    return forward, backward


def dot32(left, right):
    return jnp.dot(left, right, preferred_element_type=jnp.float32)


HBM = pltpu.HBM


def local_call(
    kernel, name, out_shape, operands, scratch=(), far_in=(), far_out=(), aliases={}
):
    outputs = out_shape if isinstance(out_shape, list) else [out_shape]
    near = pl.BlockSpec(memory_space=pltpu.VMEM)
    far = pl.BlockSpec(memory_space=HBM)
    call = pl.pallas_call(
        kernel,
        in_specs=[far if k in far_in else near for k in range(len(operands))],
        out_specs=[far if k in far_out else near for k in range(len(outputs))],
        out_shape=[
            (HBM if k in far_out else pltpu.VMEM)(o.shape, o.dtype) for k, o in enumerate(outputs)
        ],
        scratch_shapes=list(scratch),
        compiler_params=pltpu.CompilerParams(vmem_limit_bytes=8 << 20),
        input_output_aliases=aliases,
        name=name,
    )
    results = call(
        *[
            pltpu.with_memory_space_constraint(operand, HBM if k in far_in else pltpu.VMEM)
            for k, operand in enumerate(operands)
        ]
    )
    return results if isinstance(out_shape, list) else results[0]


def shape_of(shape, dtype):
    return jax.ShapeDtypeStruct(shape, dtype)


def forward_part(fwd, signal):
    count = 2 * HALF
    both = dot32(fwd, signal)
    return both[:count] + both[count:]


def joint_parts(spec, taps):
    even, cross, last = taps
    sig_even, sig_odd = spec[:HALF], spec[HALF:]
    joint = jnp.concatenate(
        [sig_even * even - sig_odd * cross, sig_even * cross + sig_odd * last], axis=0
    )
    joint_hi = joint.astype(jnp.bfloat16)
    return joint_hi, (joint - joint_hi.astype(jnp.float32)).astype(jnp.bfloat16)


def backward_part(bwd, joint_hi, joint_lo):
    back = dot32(bwd, joint_hi)
    return back[:HALF] + back[HALF:] + dot32(bwd[:HALF], joint_lo)


def gated(filtered, here, skip, query, resid):
    mixed = filtered + skip * here.astype(jnp.float32)
    return (resid.astype(jnp.float32) + query.astype(jnp.float32) * mixed).astype(jnp.bfloat16)


def filtered_result(spec, taps, here, skip, query, resid, bwd):
    return gated(backward_part(bwd, *joint_parts(spec, taps)), here, skip, query, resid)


def squares_added(total, result):
    wide = result.astype(jnp.float32)
    squares = wide * wide
    for lane in range(0, WIDE, LANES):
        part = squares[:, lane : lane + LANES]
        total = part if total is None else total + part
    return total


def write_squares(total, square_ref):
    summed = jnp.sum(total.T, axis=0, keepdims=True)
    square_ref[...] = jnp.broadcast_to(summed, square_ref.shape)


def upper_kernel(
    here_ref,
    key_far,
    value_far,
    taps_far,
    fwd_far,
    bwd_far,
    query_far,
    resid_far,
    skip_far,
    out_ref,
    square_ref,
    before_ref,
    even_ref,
    cross_ref,
    last_ref,
    key_ref,
    value_ref,
    taps_ref,
    fwd_ref,
    bwd_ref,
    query_ref,
    resid_ref,
    skip_ref,
    sems,
):
    rows = pl.ds(HALF, HALF)
    first_rows = pl.ds(0, HALF)
    copies = [
        pltpu.make_async_copy(source, target, sems.at[k])
        for k, (source, target) in enumerate(
            (
                (fwd_far, fwd_ref),
                (taps_far, taps_ref),
                (key_far.at[first_rows, :], key_ref),
                (value_far.at[first_rows, :], value_ref),
                (bwd_far, bwd_ref),
                (query_far.at[rows, :], query_ref),
                (resid_far.at[rows, :], resid_ref),
                (skip_far, skip_ref),
            )
        )
    ]
    for copy in copies:
        copy.start()
    total = None
    starts = list(range(0, here_ref.shape[1], WIDE))
    specs = {}
    for index in range(len(starts) + 2):
        if index < len(starts):
            cols = pl.ds(starts[index], WIDE)
            if index == 0:
                copies[0].wait()
                copies[1].wait()
            spec = forward_part(fwd_ref[:, :HALF], taps_ref[:, cols])
            even, odd = spec[:HALF], spec[HALF:]
            first = lax.broadcasted_iota(jnp.int32, even.shape, 0) == 0
            even_ref[:, cols] = even
            cross_ref[:, cols] = jnp.where(first, 0.0, odd)
            last_ref[:, cols] = jnp.where(first, odd, even)
        if 1 <= index <= len(starts):
            cols = pl.ds(starts[index - 1], WIDE)
            if index == 1:
                copies[2].wait()
                copies[3].wait()
            before = (
                key_ref[:, cols].astype(jnp.float32) * value_ref[:, cols].astype(jnp.float32)
            ).astype(jnp.bfloat16)
            before_ref[:, cols] = before
            signal = jnp.concatenate([before, here_ref[:, cols]], axis=0)
            specs[index - 1] = forward_part(fwd_ref[...], signal)
        if index >= 2:
            cols = pl.ds(starts[index - 2], WIDE)
            if index == 2:
                for copy in copies[4:]:
                    copy.wait()
            result = filtered_result(
                specs.pop(index - 2),
                (even_ref[:, cols], cross_ref[:, cols], last_ref[:, cols]),
                here_ref[:, cols],
                skip_ref[:, cols],
                query_ref[:, cols],
                resid_ref[:, cols],
                bwd_ref[...],
            )
            out_ref[:, cols] = result
            total = squares_added(total, result)
    write_squares(total, square_ref)


def upper_block(here, key, value, taps, tables, query, resid, skip):
    half = shape_of(here.shape, jnp.bfloat16)
    spectrum = shape_of(taps.shape, jnp.float32)
    return local_call(
        upper_kernel,
        "upper",
        [half, shape_of((SUB, HALF), jnp.float32), half, spectrum, spectrum, spectrum],
        (here, key, value, taps, *tables, query, resid, skip),
        [
            pltpu.VMEM(here.shape, jnp.bfloat16),
            pltpu.VMEM(here.shape, jnp.bfloat16),
            pltpu.VMEM(taps.shape, jnp.bfloat16),
            pltpu.VMEM(tables[0].shape, jnp.bfloat16),
            pltpu.VMEM(tables[1].shape, jnp.bfloat16),
            pltpu.VMEM(here.shape, jnp.bfloat16),
            pltpu.VMEM(here.shape, jnp.bfloat16),
            pltpu.VMEM(skip.shape, jnp.float32),
            pltpu.SemaphoreType.DMA((8,)),
        ],
        far_in=tuple(range(1, 9)),
    )


def lower_kernel(
    before_ref,
    here_ref,
    even_ref,
    cross_ref,
    last_ref,
    query_ref,
    resid_ref,
    skip_ref,
    fwd_ref,
    bwd_ref,
    out_ref,
    square_ref,
):
    rows = pl.ds(0, HALF)
    total = None
    starts = list(range(0, here_ref.shape[1], WIDE))
    specs, joints, backs = {}, {}, {}
    for index in range(len(starts) + 3):
        chunk = index - 3
        if chunk >= 0:
            cols = pl.ds(starts[chunk], WIDE)
            result = gated(
                backs.pop(chunk),
                here_ref[:, cols],
                skip_ref[:, cols],
                query_ref[rows, cols],
                resid_ref[rows, cols],
            )
            out_ref[:, cols] = result
            total = squares_added(total, result)
        chunk = index - 2
        if 0 <= chunk < len(starts):
            backs[chunk] = backward_part(bwd_ref[...], *joints.pop(chunk))
        chunk = index
        if chunk < len(starts):
            cols = pl.ds(starts[chunk], WIDE)
            signal = jnp.concatenate([before_ref[:, cols], here_ref[:, cols]], axis=0)
            specs[chunk] = forward_part(fwd_ref[...], signal)
        chunk = index - 1
        if 0 <= chunk < len(starts):
            cols = pl.ds(starts[chunk], WIDE)
            taps = (even_ref[:, cols], cross_ref[:, cols], last_ref[:, cols])
            joints[chunk] = joint_parts(specs.pop(chunk), taps)
    write_squares(total, square_ref)


def lower_block(before, here, spectrum, query, resid, skip, tables):
    return local_call(
        lower_kernel,
        "lower",
        [shape_of(here.shape, jnp.bfloat16), shape_of((SUB, HALF), jnp.float32)],
        (before, here, *spectrum, query, resid, skip, *tables),
    )


def sublane_iota():
    return lax.broadcasted_iota(jnp.int32, (SUB, LANES), 0)


def row_of(ref, row, cols):
    return jnp.broadcast_to(ref[row : row + 1, cols], (SUB, LANES))


def lane_blocks(channels, body):
    def step(pair, carry):
        for side in range(2):
            block = pair * 2 + side
            body(block, column(block), side)
        return carry

    lax.fori_loop(0, channels // (2 * LANES), step, 0)


def column(block):
    return pl.ds(pl.multiple_of(block * LANES, LANES), LANES)


def swept(wide_ref, decay_ref):
    decay = [row_of(decay_ref, m, pl.ds(0, LANES)) for m in range(decay_ref.shape[0])]
    held = None
    for i in range(STEPS):
        step = wide_ref[pl.ds(i, SUB, stride=STEPS), :]
        held = [step] * len(decay) if i == 0 else [h * d + step for h, d in zip(held, decay)]
    return held


def ready_kernel(part_ref, key_ref, gain_ref, rate_ref, scaled_ref, reach_ref):
    remaining = (sublane_iota() - (SUB - 1)).astype(jnp.float32) * float(STEPS)

    def body(block, cols, side):
        scaled_ref[:, cols] = (
            key_ref[:HALF, cols].astype(jnp.float32)
            * part_ref[:, cols].astype(jnp.float32)
            * gain_ref[:, cols]
        )
        for m in range(rate_ref.shape[0]):
            reach_ref[block, m] = jnp.exp(row_of(rate_ref, m, cols) * remaining)

    lane_blocks(rate_ref.shape[1], body)


def made_ready(part, key, gain, rates):
    modes, channels = rates.shape
    return local_call(
        ready_kernel,
        "ready",
        [
            shape_of(part.shape, jnp.float32),
            shape_of((channels // LANES, modes, SUB, LANES), jnp.float32),
        ],
        (part, key, gain, rates),
    )


def state_kernel(row_start, total_channels, last, *refs):
    if last:
        part_ref, near_ref, far_ref, rate_ref, scaled_ref, reach_ref, later_ref = refs[:7]
        value_ref, state_ref, joined_ref, wide_ref, scale_ref, decay_ref, sems = refs[8:]
        made_ref = value_ref
    else:
        part_ref, near_ref, far_ref, rate_ref, key_ref, gain_ref = refs[:6]
        value_ref, state_ref, joined_ref, end_ref = refs[6:10]
        wide_ref, scale_ref, decay_ref, sems, made_ref, held_ref = refs[10:]
    join = pltpu.make_async_copy(
        part_ref, joined_ref.at[pl.ds(row_start, HALF), :], sems.at[0]
    )
    join.start()
    modes, channels = rate_ref.shape
    rows = pl.ds(row_start, HALF)
    scale = lax.rsqrt((near_ref[...] + far_ref[...]) / total_channels + 1e-05)
    scale_ref[...] = jnp.broadcast_to(scale[:1], (HALF, HALF)).T

    def body(block, cols, side):
        decay_ref[side] = jnp.exp(-rate_ref[:, cols])
        if last:
            scaled = scaled_ref[:, cols]
        else:
            scaled = (
                key_ref[rows, cols].astype(jnp.float32)
                * part_ref[:, cols].astype(jnp.float32)
                * gain_ref[:, cols]
            )
        value = (scaled * scale_ref[...]).astype(jnp.bfloat16)
        made_ref[:, cols] = value
        wide_ref[side] = value.astype(jnp.float32)
        held = swept(wide_ref.at[side], decay_ref.at[side])
        if not last:
            for m in range(modes):
                held_ref[block, m] = held[m]
            pltpu.make_async_copy(held_ref.at[block], end_ref.at[block], sems.at[1]).start()
            pltpu.make_async_copy(made_ref.at[:, cols], value_ref.at[:, cols], sems.at[2]).start()
        remaining = (sublane_iota() - (SUB - 1)).astype(jnp.float32) * float(STEPS)
        tiles = []
        for group in range(modes // SUB):
            span = range(group * SUB, (group + 1) * SUB)
            if last:
                reach = [reach_ref[block, m] for m in span]
            else:
                reach = [jnp.exp(row_of(rate_ref, m, cols) * remaining) for m in span]
            state = gathered_sums([held[m] * r for m, r in zip(span, reach)])
            if last:
                rate = rate_ref[group * SUB : (group + 1) * SUB, cols]
                state = later_ref[group, block] + jnp.exp(-rate * float(HALF)) * state
            tiles.append(state)
        if last:
            joint = jnp.concatenate(tiles, axis=0).astype(jnp.bfloat16)
            for member in range(GROUP):
                state_ref[member, :, cols] = joint
        else:
            for group, state in enumerate(tiles):
                state_ref[group, block] = state

    lane_blocks(channels, body)
    join.wait()
    if not last:
        pltpu.make_async_copy(held_ref, end_ref, sems.at[1]).wait()
        pltpu.make_async_copy(made_ref, value_ref, sems.at[2]).wait()


def gathered_sums(values):
    row = sublane_iota()
    span = 1
    while span < SUB:
        upper = (row & span) != 0
        values = [
            jnp.where(upper, b, a) + pltpu.roll(jnp.where(upper, a, b), span, axis=0)
            for a, b in zip(values[::2], values[1::2])
        ]
        span *= 2
    return values[0]


def half_states(part, near, far, rates, extra, row_start, total_channels, last=()):
    channels = part.shape[1]
    modes = rates.shape[0]
    blocks = channels // LANES
    ends = (blocks, modes, SUB, LANES)
    outputs = [
        shape_of(part.shape, jnp.bfloat16),
        shape_of((GROUP, modes, channels), jnp.bfloat16)
        if last
        else shape_of((modes // SUB, blocks, SUB, LANES), jnp.float32),
        shape_of((2 * HALF, channels), jnp.bfloat16),
    ]
    scratch = [
        pltpu.VMEM((2, HALF, LANES), jnp.float32),
        pltpu.VMEM((HALF, HALF), jnp.float32),
        pltpu.VMEM((2, modes, LANES), jnp.float32),
        pltpu.SemaphoreType.DMA((3,)),
    ]
    if not last:
        outputs += [shape_of(ends, jnp.float32)]
        scratch += [pltpu.VMEM(part.shape, jnp.bfloat16), pltpu.VMEM(ends, jnp.float32)]
    return local_call(
        functools.partial(state_kernel, row_start, total_channels, len(last)),
        "states",
        outputs,
        (part, near, far, rates, *extra, *last),
        scratch,
        far_in=(7,) if last else (),
        far_out=(2,) if last else (0, 2, 3),
        aliases={7: 2} if last else {},
    )


def member_index():
    return lax.rem(lax.axis_index("ctx"), GROUP)


def group_kernel(span, rate_ref, state_ref, total_ref, before_ref):
    member = member_index()

    def body(block, cols, side):
        decay = jnp.exp(rate_ref[:, cols] * -span)
        held = jnp.zeros_like(decay)
        before = held
        for source in range(GROUP):
            if source > 0:
                before = jnp.where(member == source, held, before)
            held = held * decay + state_ref[source, :, cols].astype(jnp.float32)
        total = held.astype(jnp.bfloat16)
        for level in range(total_ref.shape[0]):
            total_ref[level, :, cols] = total
        before_ref[:, cols] = before

    lane_blocks(rate_ref.shape[1], body)


def group_scan(rates, states, span, levels):
    return local_call(
        functools.partial(group_kernel, float(span)),
        "group",
        [shape_of((levels, *rates.shape), jnp.bfloat16), shape_of(rates.shape, jnp.float32)],
        (rates, states),
    )


def shifted_down(value, count):
    return jnp.where(sublane_iota() >= count, pltpu.roll(value, count, axis=0), 0.0)


def tree_sum(terms):
    while len(terms) > 1:
        odd = terms[len(terms) // 2 * 2 :]
        terms = [a + b for a, b in zip(terms[::2], terms[1::2])] + odd
    return terms[0]


def weights_of(residue_ref, rate_ref):
    rates = rate_ref[...]
    return residue_ref[...] * jnp.sqrt(rates) * jnp.exp(-rates)


def inner_kernel(
    low_ref,
    far_value_ref,
    far_end_ref,
    rate_ref,
    residue_ref,
    skip_ref,
    near_ref,
    out_ref,
    weight_ref,
    wide_ref,
    decay_ref,
    tap_ref,
    made_ref,
    high_ref,
    end_ref,
    sems,
    value_sem,
    near_sem,
):
    modes, channels = rate_ref.shape
    blocks = channels // LANES

    def arriving(block):
        return pltpu.make_async_copy(far_end_ref.at[block], end_ref.at[block], sems.at[block])

    for block in range(blocks):
        arriving(block).start()
    fetch = pltpu.make_async_copy(far_value_ref, high_ref, value_sem)
    fetch.start()
    weight_ref[...] = weights_of(residue_ref, rate_ref)

    def joined(run, spans):
        for span, factor in zip((1, 2, 4), spans):
            run = run + factor * shifted_down(run, span)
        return run

    def prefix_body(block, cols, side):
        decay_ref[side] = jnp.exp(-rate_ref[:, cols])
        wide_ref[side, 0] = low_ref[:, cols].astype(jnp.float32)
        lows = swept(wide_ref.at[side, 0], decay_ref.at[side])
        arriving(block).wait()
        position = sublane_iota().astype(jnp.float32) * float(-STEPS)
        for m in range(modes):
            rate = row_of(rate_ref, m, cols)
            weight = row_of(weight_ref, m, cols)
            spans = [jnp.exp(rate * float(-STEPS * span)) for span in (1, 2, 4)]
            run = joined(lows[m], spans)
            out_ref[block, 0, m] = shifted_down(run, 1) * weight
            carried = jnp.broadcast_to(run[SUB - 1 :], (SUB, LANES))
            run = joined(end_ref[block, m], spans)
            out_ref[block, 1, m] = (
                shifted_down(run, 1) + jnp.exp(rate * position) * carried
            ) * weight

    lane_blocks(channels, prefix_body)
    fetch.wait()

    def short_body(block, cols, side):
        for start in range(0, STEPS, SUB):
            offset = (sublane_iota() + start).astype(jnp.float32)
            terms = []
            for m in range(modes):
                rate = row_of(rate_ref, m, cols)
                factor = row_of(residue_ref, m, cols) * jnp.sqrt(rate)
                terms.append(factor * jnp.exp(-rate * offset))
            tap_ref[side, start : start + SUB, :] = tree_sum(terms)
        for half, value_ref in enumerate((low_ref, high_ref)):
            wide_ref[side, half] = value_ref[:, cols].astype(jnp.float32)
            steps = [wide_ref[side, half, pl.ds(i, SUB, stride=STEPS), :] for i in range(STEPS)]
            skip = jnp.broadcast_to(skip_ref[:, cols], (SUB, LANES))
            sums = [None] * STEPS
            for k in range(STEPS):
                tap = jnp.broadcast_to(tap_ref[side, k : k + 1, :], (SUB, LANES))
                if k == 0:
                    tap = tap + skip
                for i in range(k, STEPS):
                    term = tap * steps[i - k]
                    sums[i] = term if k == 0 else sums[i] + term
            for i in range(STEPS):
                made_ref[block, pl.ds((half * STEPS + i) * SUB, SUB), :] = sums[i]
        pltpu.make_async_copy(made_ref.at[block], near_ref.at[block], near_sem).start()

    lane_blocks(channels, short_body)
    pltpu.make_async_copy(made_ref, near_ref, near_sem).wait()


def inner_part(low, high, high_end, rates, residues, skip):
    modes, channels = rates.shape
    blocks = channels // LANES
    near = shape_of((blocks, 2 * HALF, LANES), jnp.float32)
    return local_call(
        inner_kernel,
        "inner",
        [near, shape_of((blocks, 2, modes, SUB, LANES), jnp.float32)],
        (low, high, high_end, rates, residues, skip),
        [
            pltpu.VMEM(rates.shape, jnp.float32),
            pltpu.VMEM((2, 2, HALF, LANES), jnp.float32),
            pltpu.VMEM((2, modes, LANES), jnp.float32),
            pltpu.VMEM((2, STEPS, LANES), jnp.float32),
            pltpu.VMEM(near.shape, jnp.float32),
            pltpu.VMEM(high.shape, high.dtype),
            pltpu.VMEM(high_end.shape, high_end.dtype),
            pltpu.SemaphoreType.DMA((blocks,)),
            pltpu.SemaphoreType.DMA(()),
            pltpu.SemaphoreType.DMA(()),
        ],
        far_in=(1, 2),
        far_out=(0,),
    )


def output_kernel(
    lag,
    near_ref,
    prefix_ref,
    before_ref,
    totals_ref,
    rate_ref,
    residue_ref,
    query_ref,
    out_ref,
    mixed_ref,
    ready_ref,
    nears_ref,
    queries_ref,
    gain_ref,
    decay_ref,
    weight_ref,
    sems,
    out_sem,
):
    modes = rate_ref.shape[0]
    blocks = near_ref.shape[0]

    def arriving(block):
        return (
            pltpu.make_async_copy(near_ref.at[block], nears_ref.at[block], sems.at[0, block]),
            pltpu.make_async_copy(
                query_ref.at[:, column(block)], queries_ref.at[block], sems.at[1, block]
            ),
        )

    for block in range(blocks):
        for copy in arriving(block):
            copy.start()
    decay_ref[...] = jnp.exp(-rate_ref[...])
    rates = rate_ref[...]
    member = member_index().astype(jnp.float32)
    span = float(2 * HALF)
    level = jnp.exp(rates * (-span * GROUP))
    held = jnp.zeros_like(rates)
    earlier = held
    row = lax.div(lax.axis_index("ctx"), GROUP)
    for source in range(totals_ref.shape[0] - 1):
        held = held * level + totals_ref[source].astype(jnp.float32)
        earlier = jnp.where(row == source + 1, held, earlier)
    start = before_ref[...] + jnp.exp(rates * (-span * member)) * earlier
    weight_ref[...] = weights_of(residue_ref, rate_ref) * start

    def corrected(block, side):
        cols = column(block)
        every = pl.ds(0, LANES)
        for group in range(modes // SUB):
            span = slice(group * SUB, (group + 1) * SUB)
            gain = weight_ref[span, cols]
            gain_ref[side, 0, span, :] = gain
            gain_ref[side, 1, span, :] = gain * jnp.exp(rate_ref[span, cols] * float(-HALF))
        position = sublane_iota().astype(jnp.float32) * float(-STEPS)
        decay = [row_of(decay_ref, m, cols) for m in range(modes)]
        held = [[], []]
        for m in range(modes):
            reach = jnp.exp(row_of(rate_ref, m, cols) * position)
            for half in range(2):
                gain = row_of(gain_ref.at[side, half], m, every)
                held[half].append(prefix_ref[block, half, m] + reach * gain)
        for i in range(STEPS):
            for half in range(2):
                if i > 0:
                    held[half] = [h * d for h, d in zip(held[half], decay)]
                mixed_ref[block, pl.ds((half * STEPS + i) * SUB, SUB), :] = tree_sum(held[half])

    def finished(block):
        cols = column(block)
        for copy in arriving(block):
            copy.wait()
        nears_ref[block] = nears_ref[block] + mixed_ref[block]
        for half in range(2):
            for s in range(SUB):
                rows = pl.ds(half * HALF + s * STEPS, STEPS)
                mixed = nears_ref[block, pl.ds(half * HALF + s, STEPS, stride=SUB), :]
                ready_ref[rows, cols] = (
                    queries_ref[block, rows, :].astype(jnp.float32) * mixed
                ).astype(jnp.bfloat16)
        pltpu.make_async_copy(ready_ref.at[:, cols], out_ref.at[:, cols], out_sem).start()

    for block in range(lag):
        corrected(block, block % 2)

    def step(pair, carry):
        for side in range(2):
            block = lag + pair * 2 + side
            finished(block - lag)
            corrected(block, side)
        return carry

    lax.fori_loop(0, (blocks - lag) // 2, step, 0)
    for block in range(blocks - lag, blocks):
        finished(block)
    pltpu.make_async_copy(ready_ref, out_ref, out_sem).wait()


def long_output(near, prefix, before, earlier, rates, residues, query):
    blocks = near.shape[0]
    return local_call(
        functools.partial(output_kernel, 2),
        "output",
        shape_of(query.shape, jnp.bfloat16),
        (near, prefix, before, earlier, rates, residues, query),
        [
            pltpu.VMEM(near.shape, jnp.float32),
            pltpu.VMEM(query.shape, jnp.bfloat16),
            pltpu.VMEM(near.shape, jnp.float32),
            pltpu.VMEM((blocks, 2 * HALF, LANES), jnp.bfloat16),
            pltpu.VMEM((2, 2, *rates.shape[:1], LANES), jnp.float32),
            pltpu.VMEM(rates.shape, jnp.float32),
            pltpu.VMEM(rates.shape, jnp.float32),
            pltpu.SemaphoreType.DMA((2, blocks)),
            pltpu.SemaphoreType.DMA(()),
        ],
        far_in=(0, 6),
        far_out=(0,),
    )


def summed_with_pair(value):
    return value + lax.ppermute(value, "tp", [(0, 1), (1, 0), (2, 3), (3, 2)])


def across_pairs(value):
    return lax.ppermute(value, "tp", [(0, 2), (2, 0), (1, 3), (3, 1)])


def on_device(
    query_one,
    key_one,
    value_one,
    residual_in,
    medium_taps,
    skip_one,
    norm_gain,
    query_two,
    key_two,
    residues,
    decay_rates,
    skip_two,
):
    rows, channels = query_one.shape
    forward, backward = transform_tables(2 * HALF)
    tables = (
        jnp.asarray(np.concatenate(split_table(forward), axis=0)),
        jnp.asarray(np.concatenate(split_table(backward), axis=0)),
    )
    skip_row = skip_one[None, :]
    gain_row = norm_gain[None, :]
    skip_long = skip_two[None, :]
    product_high = key_one[HALF:] * value_one[HALF:]
    count = lax.axis_size("ctx")
    before = lax.ppermute(product_high, "ctx", [(d, d + 1) for d in range(count - 1)])
    high, square_high, product_low, *spectrum = upper_block(
        product_high, key_one, value_one, medium_taps, tables, query_one, residual_in, skip_row
    )
    near_high = summed_with_pair(square_high)
    far_high = across_pairs(near_high)
    total_channels = channels * lax.axis_size("tp")
    value_high, state_high, residual_out, end_high = half_states(
        high, near_high, far_high, decay_rates, (key_two, gain_row), HALF, total_channels
    )
    before, state_high = lax.optimization_barrier((before, state_high))
    low, square_low = lower_block(
        before, product_low, spectrum, query_one, residual_in, skip_row, tables
    )
    near_low = summed_with_pair(square_low)
    near_low, low = lax.optimization_barrier((near_low, low))
    far_low = across_pairs(near_low)
    ready = made_ready(low, key_two, gain_row, decay_rates)
    value_low, state, residual_out = half_states(
        low,
        near_low,
        far_low,
        decay_rates,
        ready,
        0,
        total_channels,
        (state_high, residual_out),
    )
    members = [
        [first + k for k in range(GROUP)] for first in range(0, lax.axis_size("ctx"), GROUP)
    ]
    gathered = lax.all_to_all(
        state, "ctx", split_axis=0, concat_axis=0, tiled=True, axis_index_groups=members
    )
    near, prefix = inner_part(
        value_low, value_high, end_high, decay_rates, residues, skip_long
    )
    gathered, near, prefix = lax.optimization_barrier((gathered, near, prefix))
    total, before_here = group_scan(decay_rates, gathered, rows, count // GROUP)
    columns = [list(range(first, count, GROUP)) for first in range(GROUP)]
    earlier = lax.all_to_all(
        total, "ctx", split_axis=0, concat_axis=0, tiled=True, axis_index_groups=columns
    )
    result = long_output(
        near, prefix, before_here, earlier, decay_rates, residues, query_two
    )
    return (residual_out, result)


def solution(mesh):
    in_specs = (
        P("ctx", "tp"),
        P("ctx", "tp"),
        P("ctx", "tp"),
        P("ctx", "tp"),
        P(None, "tp"),
        P("tp"),
        P("tp"),
        P("ctx", "tp"),
        P("ctx", "tp"),
        P(None, "tp"),
        P(None, "tp"),
        P("tp"),
    )
    out_specs = (P("ctx", "tp"), P("ctx", "tp"))
    return jax.shard_map(
        on_device, mesh=mesh, in_specs=in_specs, out_specs=out_specs, check_vma=False
    )
```
